512 devices in a mesh: dp: 32 (over y, z_lo), tensor: 16 (over x, z_hi, core).
Axes of the slice: x: 4, y: 4, z: 16 (z_hi: 2, z_lo: 8; z = z_hi * 8 + z_lo), core: 2. Of those that a mesh axis runs over, the one named last changes fastest.
Arguments:
- tokens: bfloat16 [16384, 4096], P(('dp', 'tensor')), may hold values from -6 to 6
- weight: bfloat16 [4096, 4096], P('tensor', 'dp'), may hold values from -0.09375 to 0.09375
Outputs:
- projected: bfloat16 [16384, 4096], P('dp', 'tensor')
The draws below stay inside these ranges and needn't reach their ends.
All inputs are finite; a program needn't handle non-finite values.
Results may differ from the reference program's by a relative error of at most 0.0057.
Values may be sent and summed in bfloat16 or wider, within the bound.
A program may use at most 64 MiB of HBM per device.

```python
import jax
import jax.numpy as jnp

D = 4096
TOKENS = 16384


def levels(rng, shape, cuts, low, high):
    level = 1.0
    for axis_at, parts in cuts:
        steps = jax.random.uniform(jax.random.fold_in(jax.random.fold_in(rng, 6), axis_at), (parts,), jnp.float32, low / len(cuts), high / len(cuts))
        level = level * jnp.repeat(jnp.exp(steps), shape[axis_at] // parts).reshape((-1,) + (1,) * (len(shape) - 1 - axis_at))
    return level


def gaussian(key, shape, width, most, shards=(), dtype=jnp.bfloat16):
    values = width * jax.random.normal(key, shape, jnp.float32)
    if shards:
        values = values * levels(key, shape, shards, -0.22, 0.18)
    return jnp.clip(values, -most, most).astype(dtype)


def setup_inputs(seed: int = 0) -> dict:
    key_list = jax.random.split(jax.random.key(seed), 3)
    tokens = gaussian(key_list[0], (TOKENS, D), 1.0, 6.0, ((0, 512),))
    weight = gaussian(key_list[1], (D, D), D ** -0.5, 0.09375, ((0, 16), (1, 32)))
    return {"tokens": tokens, "weight": weight}


def reference(tokens, weight):
    gram = jnp.dot(weight, weight.T, preferred_element_type=jnp.float32)
    gram_b = gram.astype(jnp.bfloat16)
    orthonormal = (1.5 * weight.astype(jnp.float32) - 0.5 * jnp.dot(gram_b, weight, preferred_element_type=jnp.float32)).astype(jnp.bfloat16)
    return jnp.dot(tokens, orthonormal.T, preferred_element_type=jnp.float32).astype(jnp.bfloat16)
```

```python
import functools

import jax
import jax.numpy as jnp
from jax import lax
from jax.experimental import pallas as pl
from jax.experimental.pallas import tpu as pltpu
from jax.sharding import PartitionSpec as P

MESH = pl.DeviceIdType.MESH
X, Y, H, L, C = 4, 4, 2, 8, 2
Z = H * L
B = X * H * C
LL = L // C


def dot_t(a, b):
    return lax.dot_general(a, b, (((1,), (1,)), ((), ())), preferred_element_type=jnp.float32)


def kernel(
    t_ref, w_ref, out_ref,
    zb, wc, tb, pf, pr, ys, yr, gb, ob, oc, acc,
    loc, s_z, r_z, s_x, s_w, r_w, s_p, r_p, s_y, r_y, s_g, s_h, r_g,
    s_l, r_l, s_o, s_c, s_r, r_o, s_t, s_u, r_t,
):
    dp, tn = lax.axis_index("dp"), lax.axis_index("tensor")
    y, l = lax.div(dp, L), lax.rem(dp, L)
    x, h, c = lax.div(tn, H * C), lax.rem(lax.div(tn, C), H), lax.rem(tn, C)
    z = h * L + l
    other = 1 - c
    rb, cb = w_ref.shape
    rows = t_ref.shape[0]
    cw = LL * cb
    r = rb // LL

    def dev(ax, ay, az, ac):
        return (ay * L + lax.rem(az, L), (ax * H + lax.div(az, L)) * C + ac)

    def xs(k):
        return lax.rem(x + k, X)

    def yy(k):
        return lax.rem(y + k, Y)

    def zz(k):
        return lax.rem(z + k, Z)

    def send(src, dst, ssem, rsem, device):
        return pltpu.make_async_remote_copy(
            src_ref=src, dst_ref=dst, send_sem=ssem, recv_sem=rsem, device_id=device, device_id_type=MESH
        )

    def await_copy(ref, sem):
        pltpu.make_async_copy(ref, ref, sem).wait()

    def blk(ax, ah, ac):
        return (ax * H + ah) * C + ac

    def tblk(b):
        return tb.at[pl.ds(pl.multiple_of(b * rows, rows), rows), :]

    mine = blk(x, h, c)
    load_w = pltpu.make_async_copy(w_ref, zb.at[z], loc.at[0])
    load_t = pltpu.make_async_copy(t_ref, tblk(mine), loc.at[1])
    load_w.start()
    load_t.start()

    barrier = pltpu.get_barrier_semaphore()
    peers = [dev(x, y, zz(1), c), dev(x, y, zz(Z - 1), c), dev(x, y, zz(L), c), dev(x, y, z, other)]
    peers += [dev(xs(k), y, z, a) for k in (1, X - 1) for a in (c, other)]
    peers += [dev(x, yy(k), z, a) for k in (1, Y - 1) for a in (c, other)] + [dev(x, yy(2), z, c)]
    for peer in peers:
        pl.semaphore_signal(barrier, inc=1, device_id=peer, device_id_type=MESH)
    pl.semaphore_wait(barrier, len(peers))
    load_w.wait()
    load_t.wait()

    def slot(b, k):
        return wc.at[b, :, pl.ds(pl.multiple_of(k * cb, cb), cb)]

    def up(q, i):
        send(zb.at[q], zb.at[q], s_z.at[0], r_z.at[q], dev(x, y, zz(1), c)).start()

    def down(q, i):
        send(zb.at[q], zb.at[q], s_z.at[1], r_z.at[q], dev(x, y, zz(Z - 1), c)).start()

    def spread(q):
        lq = lax.rem(q, L)
        to, k = lax.div(lq, LL), lax.rem(lq, LL)
        b = blk(x, lax.div(q, L), c)
        sem = r_w.at[b, k]
        send(zb.at[q], slot(b, k), s_x.at[0], sem, dev(xs(1), y, z, to)).start()
        send(zb.at[q], slot(b, k), s_x.at[1], sem, dev(xs(X - 1), y, z, to)).start()

        @pl.when(to != c)
        def _():
            send(zb.at[q], slot(b, k), s_x.at[2], sem, dev(x, y, z, other)).start()

        @pl.when(to == c)
        def _():
            pltpu.make_async_copy(zb.at[q], slot(b, k), sem).start()

    def relay(q):
        lq = lax.rem(q, L)
        k, hq = lax.rem(lq, LL), lax.div(q, L)

        @pl.when(lax.div(lq, LL) == c)
        def _():
            even = lax.rem(q, 2) == 0
            near = jnp.where(even, xs(X - 1), xs(1))
            far = jnp.where(even, xs(1), xs(X - 1))
            for a in range(C):
                b = blk(near, hq, a)
                await_copy(slot(b, k), r_w.at[b, k])
                send(slot(b, k), slot(b, k), s_w, r_w.at[b, k], dev(far, y, z, c)).start()

    up(z, 0)
    down(z, 0)
    spread(z)

    def z_step(s, _):
        q = zz(Z - s)
        await_copy(zb.at[q], r_z.at[q])
        up(q, s)
        p = zz(s)
        await_copy(zb.at[p], r_z.at[p])

        @pl.when(s < Z // 2 - 1)
        def _():
            down(p, s)

        spread(q)
        spread(p)

        @pl.when(s == 2)
        def _():
            relay(z)

        @pl.when(s > 2)
        def _():
            relay(zz(Z - s + 2))
            relay(zz(s - 2))

        return 0

    lax.fori_loop(1, Z // 2, z_step, 0)
    q = zz(Z // 2)
    await_copy(zb.at[q], r_z.at[q])
    spread(q)
    partner = blk(x, 1 - h, c)
    send(tblk(mine), tblk(mine), s_t.at[0], r_t.at[mine], dev(x, y, zz(L), c)).start()
    for s in (Z // 2 - 2, Z // 2 - 1):
        relay(zz(Z - s))
        relay(zz(s))
    relay(q)

    def t_spread(b):
        send(tblk(b), tblk(b), s_u.at[0], r_t.at[b], dev(xs(1), y, z, c)).start()
        send(tblk(b), tblk(b), s_u.at[1], r_t.at[b], dev(xs(X - 1), y, z, c)).start()

    def t_other(b):
        send(tblk(b), tblk(b), s_u.at[3], r_t.at[b], dev(x, y, z, other)).start()

    t_spread(mine)

    def rest(i, _):
        hq, k, a = lax.div(i, LL * C), lax.rem(lax.div(i, C), LL), lax.rem(i, C)
        q = hq * L + c * LL + k
        near = jnp.where(lax.rem(q, 2) == 0, xs(1), xs(X - 1))
        for ax in (x, xs(2), near):
            b = blk(ax, hq, a)
            await_copy(slot(b, k), r_w.at[b, k])
        return 0

    lax.fori_loop(0, H * LL * C, rest, 0)

    half = B // C
    own = blk(x, h, lax.div(l, LL))
    wr = wc[own, pl.ds(pl.multiple_of(lax.rem(l, LL) * r, r), r), :]

    def gram(i, _):
        b = lax.rem(other * half + i, B)
        pf[b] = dot_t(wr, wc[b])
        return 0

    lax.fori_loop(0, half, gram, 0)
    half_copy = send(pf.at[pl.ds(other * half, half)], pr, s_p, r_p, dev(x, y, z, other))
    half_copy.start()
    lax.fori_loop(half, B, gram, 0)
    half_copy.wait_recv()
    per = half // Y

    def fold(i, _):
        total = pf[c * half + i] + pr[i]
        pf[c * half + i] = total
        ys[i] = total.astype(jnp.bfloat16)
        return 0

    lax.fori_loop(0, half, fold, 0)
    for k in (2, 1, Y - 1):
        send(ys.at[pl.ds(yy(k) * per, per)], yr.at[k], s_y.at[k], r_y.at[k], dev(x, yy(k), z, c)).start()
    for k in (1, Y - 1, 2):
        await_copy(yr.at[k], r_y.at[k])
    for j in range(per):
        i = y * per + j
        total = pf[c * half + i]
        for k in range(1, Y):
            total = total + yr[k, j].astype(jnp.float32)
        gb[c * half + i] = total.astype(jnp.bfloat16)

    def g_at(a, k):
        return gb.at[pl.ds(a * half + k * per, per)]

    for k in (2, 1, Y - 1):
        send(g_at(c, y), g_at(c, y), s_g.at[k], r_g.at[c, y], dev(x, yy(k), z, c)).start()
    send(g_at(c, y), g_at(c, y), s_h.at[0], r_g.at[c, y], dev(x, y, z, other)).start()
    for k in (1, Y - 1, 2):
        await_copy(g_at(c, yy(k)), r_g.at[c, yy(k)])
        send(g_at(c, yy(k)), g_at(c, yy(k)), s_h.at[k], r_g.at[c, yy(k)], dev(x, y, z, other)).start()
    for k in range(Y):
        await_copy(g_at(other, yy(k)), r_g.at[other, yy(k)])

    acc_o = 1.5 * wr.astype(jnp.float32)

    def update(b, total):
        return total - 0.5 * jnp.dot(gb[b], wc[b], preferred_element_type=jnp.float32)

    ob[l] = lax.fori_loop(0, B, update, acc_o).astype(jnp.bfloat16)

    def o_slot(a, k):
        return oc.at[a, pl.ds(pl.multiple_of(k * r, r), r), :]

    def o_up(q):
        @pl.when(l < L - 1)
        def _():
            send(ob.at[q], ob.at[q], s_l.at[0, q], r_l.at[q], (dp + 1, tn)).start()

    def o_down(q):
        @pl.when(l > 0)
        def _():
            send(ob.at[q], ob.at[q], s_l.at[1, q], r_l.at[q], (dp - 1, tn)).start()

    def o_spread(q):
        to, k = lax.div(q, LL), lax.rem(q, LL)
        a = y * C + c
        send(ob.at[q], o_slot(a, k), s_o.at[0], r_o.at[a, k], dev(x, yy(1), z, to)).start()
        send(ob.at[q], o_slot(a, k), s_o.at[1], r_o.at[a, k], dev(x, yy(Y - 1), z, to)).start()

        @pl.when(to != c)
        def _():
            send(ob.at[q], o_slot(a, k), s_c, r_o.at[a, k], dev(x, y, z, other)).start()

        @pl.when(to == c)
        def _():
            pltpu.make_async_copy(ob.at[q], o_slot(a, k), r_o.at[a, k]).start()

    def o_relay(q):
        @pl.when(lax.div(q, LL) == c)
        def _():
            k = lax.rem(q, LL)
            for a, near, far in ((yy(Y - 1) * C, yy(Y - 1), yy(1)), (yy(1) * C + 1, yy(1), yy(Y - 1))):
                await_copy(o_slot(a, k), r_o.at[a, k])
                send(o_slot(a, k), o_slot(a, k), s_r, r_o.at[a, k], dev(x, far, z, c)).start()

    o_up(l)
    o_down(l)
    o_spread(l)

    await_copy(tblk(partner), r_t.at[partner])
    t_spread(partner)
    t_other(mine)
    t_other(partner)

    def l_step(s, _):
        @pl.when(l - s >= 0)
        def _():
            await_copy(ob.at[l - s], r_l.at[l - s])
            o_up(l - s)
            o_spread(l - s)

        @pl.when(l + s < L)
        def _():
            await_copy(ob.at[l + s], r_l.at[l + s])
            o_down(l + s)
            o_spread(l + s)

        @pl.when(s == 2)
        def _():
            o_relay(l)

        @pl.when((s > 2) & (l - s + 2 >= 0))
        def _():
            o_relay(l - s + 2)

        @pl.when((s > 2) & (l + s - 2 < L))
        def _():
            o_relay(l + s - 2)

        return 0

    lax.fori_loop(1, L, l_step, 0)

    for hq, near, far in ((0, xs(X - 1), xs(1)), (1, xs(1), xs(X - 1))):
        b = blk(near, hq, c)
        await_copy(tblk(b), r_t.at[b])
        send(tblk(b), tblk(b), s_u.at[2], r_t.at[b], dev(far, y, z, c)).start()
        t_other(b)
    for hq, near in ((1, xs(X - 1)), (0, xs(1))):
        b = blk(near, hq, c)
        await_copy(tblk(b), r_t.at[b])
        t_other(b)

    for s in (L - 2, L - 1):
        @pl.when(l - s >= 0)
        def _():
            o_relay(l - s)

        @pl.when(l + s < L)
        def _():
            o_relay(l + s)

    for hq in range(H):
        b = blk(xs(2), hq, c)
        await_copy(tblk(b), r_t.at[b])
        t_other(b)
    for k in range(X):
        for hq in range(H):
            b = blk(xs(k), hq, other)
            await_copy(tblk(b), r_t.at[b])

    def o_rest(k, _):
        for a in (y * C, y * C + 1, yy(2) * C, yy(2) * C + 1, yy(Y - 1) * C + 1, yy(1) * C):
            await_copy(o_slot(a, k), r_o.at[a, k])
        return 0

    lax.fori_loop(0, LL, o_rest, 0)

    acc[...] = jnp.zeros_like(acc)

    def project(a, _):
        acc[...] += dot_t(tb[:, pl.ds(pl.multiple_of(a * cw, cw), cw)], oc[a])
        return 0

    lax.fori_loop(0, Y * C, project, 0)
    out_ref[...] = acc[...].astype(jnp.bfloat16)

    def sent(ref, sem):
        pltpu.make_async_copy(ref, ref, sem).wait()

    sent(zb.at[pl.ds(0, Z // 2)], s_z.at[0])
    sent(zb.at[pl.ds(0, Z // 2 - 1)], s_z.at[1])
    sent(zb, s_x.at[0])
    sent(zb, s_x.at[1])
    sent(zb.at[pl.ds(0, Z // 2)], s_x.at[2])
    sent(zb, s_w)
    half_copy.wait_send()
    for k in range(1, Y):
        sent(yr.at[k], s_y.at[k])
        sent(yr.at[k], s_g.at[k])
    for k in range(Y):
        sent(yr.at[0], s_h.at[k])
    sent(tblk(mine), s_t.at[0])
    two, eight = tb.at[pl.ds(0, H * rows), :], tb.at[pl.ds(0, X * H * rows), :]
    sent(two, s_u.at[0])
    sent(two, s_u.at[1])
    sent(two, s_u.at[2])
    sent(eight, s_u.at[3])
    sent(ob, s_o.at[0])
    sent(ob, s_o.at[1])
    sent(ob.at[pl.ds(0, L // 2)], s_c)
    sent(ob, s_r)

    def line(q, _):
        @pl.when((l < L - 1) & (q <= l))
        def _():
            sent(ob.at[q], s_l.at[0, q])

        @pl.when((l > 0) & (q >= l))
        def _():
            sent(ob.at[q], s_l.at[1, q])

        return 0

    lax.fori_loop(0, L, line, 0)


def on_device(tokens, weight):
    rows, d = tokens.shape
    rb, cb = weight.shape
    cw, r, half = LL * cb, rb // LL, B // C
    dma = pltpu.SemaphoreType.DMA
    bf, f32 = jnp.bfloat16, jnp.float32
    return pl.pallas_call(
        kernel,
        out_shape=jax.ShapeDtypeStruct((B * rows, rb), bf),
        in_specs=[pl.BlockSpec(memory_space=pl.ANY)] * 2,
        out_specs=pl.BlockSpec(memory_space=pltpu.VMEM),
        scratch_shapes=[
            pltpu.VMEM((Z, rb, cb), bf),
            pltpu.VMEM((B, rb, cw), bf),
            pltpu.VMEM((B * rows, d), bf),
            pltpu.VMEM((B, r, rb), f32),
            pltpu.VMEM((half, r, rb), f32),
            pltpu.VMEM((half, r, rb), bf),
            pltpu.VMEM((Y, half // Y, r, rb), bf),
            pltpu.VMEM((B, r, rb), bf),
            pltpu.VMEM((L, r, cw), bf),
            pltpu.VMEM((Y * C, rb, cw), bf),
            pltpu.VMEM((B * rows, rb), f32),
            dma((2,)),
            dma((2,)), dma((Z,)), dma((3,)), dma, dma((B, LL)),
            dma, dma, dma((Y,)), dma((Y,)), dma((Y,)), dma((Y,)), dma((C, Y)),
            dma((2, L)), dma((L,)), dma((2,)), dma, dma, dma((Y * C, LL)),
            dma((1,)), dma((4,)), dma((B,)),
        ],
        compiler_params=pltpu.CompilerParams(
            collective_id=0, has_side_effects=True, vmem_limit_bytes=48 * 1024 * 1024
        ),
        name="bjorck",
    )(tokens, weight)


def solution(mesh):
    placed = (P(("dp", "tensor"), None), P("tensor", "dp"))
    return jax.shard_map(
        on_device, mesh=mesh, in_specs=placed, out_specs=P("dp", "tensor"), check_vma=False
    )
```

```python
import functools

import jax
import jax.numpy as jnp
from jax import lax
from jax.experimental import pallas as pl
from jax.experimental.pallas import tpu as pltpu
from jax.sharding import PartitionSpec as P

MESH = pl.DeviceIdType.MESH
X, Y, H, L, C = 4, 4, 2, 8, 2
Z = H * L
B = X * H * C
LL = L // C
NC, FC = 2, 2


def dot_t(a, b):
    return lax.dot_general(a, b, (((1,), (1,)), ((), ())), preferred_element_type=jnp.float32)


def kernel(
    t_ref, w_ref, out_ref,
    zb, wc, rr, tb, t4, pf, pr, ys, yr, gb, po, xb, xr, ob, oc, acc,
    loc, s_z, r_z, s_x, s_m, r_m, r_w, s_p, r_p, s_y, r_y, s_g, s_h, r_g, s_q, r_q,
    s_l, r_l, s_o, s_c, s_r, r_o, s_t, r_t4, r_tp, s_u, r_t,
):
    dp, tn = lax.axis_index("dp"), lax.axis_index("tensor")
    y, l = lax.div(dp, L), lax.rem(dp, L)
    x, h, c = lax.div(tn, H * C), lax.rem(lax.div(tn, C), H), lax.rem(tn, C)
    z = h * L + l
    other = 1 - c
    rb, cb = w_ref.shape
    rows = t_ref.shape[0]
    cw = LL * cb
    r = rb // LL
    zr, fr, tr = rb // NC, r // FC, rows // 2

    def dev(ax, ay, az, ac):
        return (ay * L + lax.rem(az, L), (ax * H + lax.div(az, L)) * C + ac)

    def xs(k):
        return lax.rem(x + k, X)

    def yy(k):
        return lax.rem(y + k, Y)

    def zz(k):
        return lax.rem(z + k, Z)

    def send(src, dst, ssem, rsem, device):
        return pltpu.make_async_remote_copy(
            src_ref=src, dst_ref=dst, send_sem=ssem, recv_sem=rsem, device_id=device, device_id_type=MESH
        )

    def await_copy(ref, sem):
        pltpu.make_async_copy(ref, ref, sem).wait()

    def blk(ax, ah, ac):
        return (ax * H + ah) * C + ac

    def tblk(b):
        return tb.at[pl.ds(pl.multiple_of(b * rows, rows), rows), :]

    def thalf(b, i):
        return tb.at[pl.ds(pl.multiple_of(b * rows + i * tr, tr), tr), :]

    def part(ref, i):
        return ref.at[pl.ds(pl.multiple_of(i * r, r), r), :]

    mine, partner = blk(x, h, c), blk(x, 1 - h, c)
    loads = [pltpu.make_async_copy(w_ref.at[pl.ds(i * zr, zr), :], zb.at[z, i], loc.at[i]) for i in range(NC)]
    loads.append(pltpu.make_async_copy(t_ref, tblk(mine), loc.at[NC]))
    for load in loads:
        load.start()

    barrier = pltpu.get_barrier_semaphore()
    peers = [dev(x, y, zz(1), c), dev(x, y, zz(Z - 1), c), dev(x, y, z, other)]
    peers += [dev(xs(k), y, z, a) for k in (1, 2, 3) for a in (c, other)]
    peers += [dev(x, yy(k), z, a) for k in (1, Y - 1) for a in (c, other)] + [dev(x, yy(2), z, c)]
    for peer in peers:
        pl.semaphore_signal(barrier, inc=1, device_id=peer, device_id_type=MESH)
    pl.semaphore_wait(barrier, len(peers))
    for load in loads:
        load.wait()

    own_core, own_row = lax.div(l, LL), lax.rem(l, LL) * r
    own_chunk = lax.div(own_row, zr)

    def slot(b, i, k):
        return wc.at[b, pl.ds(i * zr, zr), pl.ds(pl.multiple_of(k * cb, cb), cb)]

    def up(q, i, sem=0):
        send(zb.at[q, i], zb.at[q, i], s_z.at[sem], r_z.at[q, i], dev(x, y, zz(1), c)).start()

    def down(q, i, sem=1):
        send(zb.at[q, i], zb.at[q, i], s_z.at[sem], r_z.at[q, i], dev(x, y, zz(Z - 1), c)).start()

    def spread(q, i):
        lq, hq = lax.rem(q, L), lax.div(q, L)
        to, k = lax.div(lq, LL), lax.rem(lq, LL)
        b = hq * C + c

        @pl.when((hq == h) & (own_core == c) & (own_chunk == i))
        def _():
            src = zb.at[q, i, pl.ds(pl.multiple_of(own_row - i * zr, r), r), :]
            dst = rr.at[pl.ds(pl.multiple_of(x * r, r), r), pl.ds(pl.multiple_of(k * cb, cb), cb)]
            for n in (2, 1, 3):
                send(src, dst, s_m, r_m.at[x, k], dev(xs(n), y, z, to)).start()

        @pl.when(to != c)
        def _():
            send(zb.at[q, i], slot(b, i, k), s_x, r_w.at[b, i, k], dev(x, y, z, other)).start()

        @pl.when(to == c)
        def _():
            pltpu.make_async_copy(zb.at[q, i], slot(b, i, k), r_w.at[b, i, k]).start()
    for i in range(NC):
        up(z, i)
        down(z, i)
    for i in range(NC):
        spread(z, i)

    def z_step(s, _):
        q, p = zz(Z - s), zz(s)
        for i in range(NC):
            await_copy(zb.at[q, i], r_z.at[q, i])
            up(q, i)
            await_copy(zb.at[p, i], r_z.at[p, i])
            down(p, i)
        for i in range(NC):
            spread(q, i)
            spread(p, i)
        return 0
    lax.fori_loop(1, Z // 2 - 1, z_step, 0)
    q, p = zz(Z // 2 + 1), zz(Z // 2 - 1)
    for i in range(NC):
        await_copy(zb.at[q, i], r_z.at[q, i])
        if i < NC // 2:
            up(q, i, 2)
        await_copy(zb.at[p, i], r_z.at[p, i])
        if i >= NC // 2:
            down(p, i, 3)
    for i in range(NC):
        spread(q, i)
        spread(p, i)

    def t_spread(b):
        send(tblk(b), tblk(b), s_u.at[0], r_t.at[b], dev(xs(1), y, z, c)).start()
        send(tblk(b), tblk(b), s_u.at[1], r_t.at[b], dev(xs(X - 1), y, z, c)).start()

    def t_other(b):
        send(tblk(b), tblk(b), s_u.at[3], r_t.at[b], dev(x, y, z, other)).start()

    quarter = Z // 4
    q = zz(Z // 2)
    for i in range(NC):
        await_copy(zb.at[q, i], r_z.at[q, i])
        spread(q, i)
    send(thalf(mine, 0), t4.at[0], s_t.at[0], r_t4.at[0], dev(x, y, zz(quarter), c)).start()
    send(thalf(mine, 1), t4.at[1], s_t.at[1], r_t4.at[1], dev(x, y, zz(Z - quarter), c)).start()
    for b in range(H * C):
        for i in range(NC):
            for k in range(LL):
                await_copy(slot(b, i, k), r_w.at[b, i, k])
    for n in (1, 2, 3):
        for k in range(LL):
            await_copy(
                rr.at[pl.ds(pl.multiple_of(xs(n) * r, r), r), pl.ds(k * cb, cb)], r_m.at[xs(n), k]
            )
    t_spread(mine)
    t_other(mine)

    half = H * C // C
    wr = wc[h * C + own_core, pl.ds(pl.multiple_of(own_row, r), r), :]
    rr[pl.ds(pl.multiple_of(x * r, r), r), :] = wr
    for i in range(half):
        b = other * half + i
        pf[b] = dot_t(rr[...], wc[b])
    half_copy = send(pf.at[pl.ds(other * half, half)], pr, s_p, r_p, dev(x, y, z, other))
    half_copy.start()
    for i in range(half):
        b = c * half + i
        pf[b] = dot_t(rr[...], wc[b])
    half_copy.wait_recv()
    for i in range(half):
        total = pf[c * half + i] + pr[i]
        pf[c * half + i] = total
        ys[i] = total.astype(jnp.bfloat16)

    def y_part(ref, k):
        return ref.at[:, pl.ds(pl.multiple_of(k * r, r), r), :]

    for k in (2, 1, Y - 1):
        send(y_part(ys, yy(k)), yr.at[k], s_y.at[k], r_y.at[k], dev(x, yy(k), z, c)).start()
    for k in (1, Y - 1, 2):
        await_copy(yr.at[k], r_y.at[k])
    my_rows = pl.ds(pl.multiple_of(y * r, r), r)
    for i in range(half):
        total = pf[c * half + i, my_rows, :]
        for k in range(1, Y):
            total = total + yr[k, i].astype(jnp.float32)
        gb[c * half + i, my_rows, :] = total.astype(jnp.bfloat16)

    def g_at(a, k):
        return gb.at[pl.ds(a * half, half), pl.ds(pl.multiple_of(k * r, r), r), :]
    for k in (2, 1, Y - 1):
        send(g_at(c, y), g_at(c, y), s_g.at[k], r_g.at[c, y], dev(x, yy(k), z, c)).start()
    send(g_at(c, y), g_at(c, y), s_h.at[0], r_g.at[c, y], dev(x, y, z, other)).start()
    for k in (1, Y - 1, 2):
        await_copy(g_at(c, yy(k)), r_g.at[c, yy(k)])
        send(g_at(c, yy(k)), g_at(c, yy(k)), s_h.at[k], r_g.at[c, yy(k)], dev(x, y, z, other)).start()
    for i, ahead, back in ((0, quarter, Z - quarter), (1, Z - quarter, quarter)):
        await_copy(t4.at[i], r_t4.at[i])
        home = blk(x, lax.div(zz(back), L), c)
        send(t4.at[i], thalf(home, i), s_t.at[2 + i], r_tp.at[i], dev(x, y, zz(ahead), c)).start()
    for k in range(Y):
        await_copy(g_at(other, yy(k)), r_g.at[other, yy(k)])

    total = jnp.dot(gb[0], wc[0], preferred_element_type=jnp.float32)
    for b in range(1, H * C):
        total = total + jnp.dot(gb[b], wc[b], preferred_element_type=jnp.float32)
    total = -0.5 * total
    po[...] = total
    xb[...] = total.astype(jnp.bfloat16)
    for n in (2, 1, 3):
        send(part(xb, xs(n)), xr.at[n], s_q.at[n], r_q.at[n], dev(xs(n), y, z, c)).start()
    for n in (1, 3, 2):
        await_copy(xr.at[n], r_q.at[n])
    total = 1.5 * wr.astype(jnp.float32) + po[pl.ds(pl.multiple_of(x * r, r), r), :]
    for n in (1, 2, 3):
        total = total + xr[n].astype(jnp.float32)
    for i in range(FC):
        ob[l, i] = total[i * fr:(i + 1) * fr].astype(jnp.bfloat16)

    def o_slot(a, k, i):
        return oc.at[a, pl.ds(pl.multiple_of(k * r + i * fr, fr), fr), :]

    def o_up(q, i):
        @pl.when(l < L - 1)
        def _():
            send(ob.at[q, i], ob.at[q, i], s_l.at[0, q], r_l.at[q, i], (dp + 1, tn)).start()

    def o_down(q, i):
        @pl.when(l > 0)
        def _():
            send(ob.at[q, i], ob.at[q, i], s_l.at[1, q], r_l.at[q, i], (dp - 1, tn)).start()

    def o_spread(q, i):
        to, k = lax.div(q, LL), lax.rem(q, LL)
        a = y * C + c
        dst, sem = o_slot(a, k, i), r_o.at[a, k, i]
        send(ob.at[q, i], dst, s_o.at[0], sem, dev(x, yy(1), z, to)).start()
        send(ob.at[q, i], dst, s_o.at[1], sem, dev(x, yy(Y - 1), z, to)).start()

        @pl.when(to != c)
        def _():
            send(ob.at[q, i], dst, s_c, sem, dev(x, y, z, other)).start()

        @pl.when(to == c)
        def _():
            pltpu.make_async_copy(ob.at[q, i], dst, sem).start()

    def o_relay(q):
        @pl.when(lax.div(q, LL) == c)
        def _():
            k = lax.rem(q, LL)
            for i in range(FC):
                for a, far in ((yy(Y - 1) * C, yy(1)), (yy(1) * C + 1, yy(Y - 1))):
                    await_copy(o_slot(a, k, i), r_o.at[a, k, i])
                    send(o_slot(a, k, i), o_slot(a, k, i), s_r, r_o.at[a, k, i], dev(x, far, z, c)).start()
    for i in range(FC):
        o_up(l, i)
        o_down(l, i)
    for i in range(FC):
        o_spread(l, i)

    def t_pass(hq, a, b):
        near = blk(a, hq, c)
        await_copy(tblk(near), r_t.at[near])
        send(tblk(near), tblk(near), s_u.at[2], r_t.at[near], dev(b, y, z, c)).start()
        t_other(near)

    def t_turn(hq):
        @pl.when(hq == 0)
        def _():
            t_pass(0, xs(X - 1), xs(1))

        @pl.when(hq == 1)
        def _():
            t_pass(1, xs(1), xs(X - 1))
    t_turn(h)

    def l_step(s, _):
        for i in range(FC):
            @pl.when(l - s >= 0)
            def _():
                await_copy(ob.at[l - s, i], r_l.at[l - s, i])
                o_up(l - s, i)

            @pl.when(l + s < L)
            def _():
                await_copy(ob.at[l + s, i], r_l.at[l + s, i])
                o_down(l + s, i)

        for i in range(FC):
            @pl.when(l - s >= 0)
            def _():
                o_spread(l - s, i)

            @pl.when(l + s < L)
            def _():
                o_spread(l + s, i)

        @pl.when(s == 2)
        def _():
            o_relay(l)

        @pl.when((s > 2) & (l - s + 2 >= 0))
        def _():
            o_relay(l - s + 2)

        @pl.when((s > 2) & (l + s - 2 < L))
        def _():
            o_relay(l + s - 2)

        @pl.when(s == 2)
        def _():
            await_copy(thalf(partner, 0), r_tp.at[0])
            await_copy(thalf(partner, 1), r_tp.at[1])
            t_spread(partner)
            t_other(partner)

        @pl.when(s == 5)
        def _():
            t_turn(1 - h)

        return 0
    lax.fori_loop(1, L, l_step, 0)
    for s in (L - 2, L - 1):
        @pl.when(l - s >= 0)
        def _():
            o_relay(l - s)

        @pl.when(l + s < L)
        def _():
            o_relay(l + s)
    for hq, a in ((1, xs(X - 1)), (0, xs(1)), (0, xs(2)), (1, xs(2))):
        b = blk(a, hq, c)
        await_copy(tblk(b), r_t.at[b])
        t_other(b)
    for k in range(X):
        for hq in range(H):
            b = blk(xs(k), hq, other)
            await_copy(tblk(b), r_t.at[b])

    def o_rest(k, _):
        for i in range(FC):
            for a in (y * C, y * C + 1, yy(2) * C, yy(2) * C + 1, yy(Y - 1) * C + 1, yy(1) * C):
                await_copy(o_slot(a, k, i), r_o.at[a, k, i])
        return 0
    lax.fori_loop(0, LL, o_rest, 0)
    acc[...] = jnp.zeros_like(acc)

    def project(a, _):
        acc[...] += dot_t(tb[:, pl.ds(pl.multiple_of(a * cw, cw), cw)], oc[a])
        return 0

    lax.fori_loop(0, Y * C, project, 0)
    out_ref[...] = acc[...].astype(jnp.bfloat16)

    def sent(ref, sem):
        pltpu.make_async_copy(ref, ref, sem).wait()
    for n in range(2):
        sent(zb.at[pl.ds(0, Z // 2 - 1)], s_z.at[n])
        sent(zb.at[0, pl.ds(0, NC // 2)], s_z.at[2 + n])
    sent(zb.at[pl.ds(0, Z // 2)], s_x)

    @pl.when(own_core == c)
    def _():
        sent(zb.at[pl.ds(0, L * 3 // LL)], s_m)

    half_copy.wait_send()
    for k in range(1, Y):
        sent(yr.at[k], s_y.at[k])
        sent(yr.at[k], s_g.at[k])
        sent(xr.at[k], s_q.at[k])
    for k in range(Y):
        sent(yr.at[0], s_h.at[k])
    for k in range(4):
        sent(t4.at[0], s_t.at[k])
    two, eight = tb.at[pl.ds(0, H * rows), :], tb.at[pl.ds(0, X * H * rows), :]
    sent(two, s_u.at[0])
    sent(two, s_u.at[1])
    sent(two, s_u.at[2])
    sent(eight, s_u.at[3])
    sent(ob, s_o.at[0])
    sent(ob, s_o.at[1])
    sent(ob.at[pl.ds(0, L // 2)], s_c)
    sent(ob, s_r)

    def line(q, _):
        @pl.when((l < L - 1) & (q <= l))
        def _():
            sent(ob.at[q], s_l.at[0, q])

        @pl.when((l > 0) & (q >= l))
        def _():
            sent(ob.at[q], s_l.at[1, q])

        return 0

    lax.fori_loop(0, L, line, 0)


def on_device(tokens, weight):
    rows, d = tokens.shape
    rb, cb = weight.shape
    cw, r, half = LL * cb, rb // LL, H
    dma = pltpu.SemaphoreType.DMA
    bf, f32 = jnp.bfloat16, jnp.float32
    return pl.pallas_call(
        kernel,
        out_shape=jax.ShapeDtypeStruct((B * rows, rb), bf),
        in_specs=[pl.BlockSpec(memory_space=pl.ANY)] * 2,
        out_specs=pl.BlockSpec(memory_space=pltpu.VMEM),
        scratch_shapes=[
            pltpu.VMEM((Z, NC, rb // NC, cb), bf),
            pltpu.VMEM((H * C, rb, cw), bf),
            pltpu.VMEM((X * r, cw), bf),
            pltpu.VMEM((B * rows, d), bf),
            pltpu.VMEM((2, rows // 2, d), bf),
            pltpu.VMEM((H * C, X * r, rb), f32),
            pltpu.VMEM((half, X * r, rb), f32),
            pltpu.VMEM((half, X * r, rb), bf),
            pltpu.VMEM((Y, half, r, rb), bf),
            pltpu.VMEM((H * C, X * r, rb), bf),
            pltpu.VMEM((X * r, cw), f32),
            pltpu.VMEM((X * r, cw), bf),
            pltpu.VMEM((X, r, cw), bf),
            pltpu.VMEM((L, FC, r // FC, cw), bf),
            pltpu.VMEM((Y * C, rb, cw), bf),
            pltpu.VMEM((B * rows, rb), f32),
            dma((NC + 1,)),
            dma((4,)), dma((Z, NC)), dma, dma, dma((X, LL)), dma((H * C, NC, LL)),
            dma, dma, dma((Y,)), dma((Y,)), dma((Y,)), dma((Y,)), dma((C, Y)), dma((X,)), dma((X,)),
            dma((2, L)), dma((L, FC)), dma((2,)), dma, dma, dma((Y * C, LL, FC)),
            dma((4,)), dma((2,)), dma((2,)), dma((4,)), dma((B,)),
        ],
        compiler_params=pltpu.CompilerParams(
            collective_id=0, has_side_effects=True, vmem_limit_bytes=64_000_000
        ),
        name="bjorck",
    )(tokens, weight)


def solution(mesh):
    placed = (P(("dp", "tensor"), None), P("tensor", "dp"))
    return jax.shard_map(
        on_device, mesh=mesh, in_specs=placed, out_specs=P("dp", "tensor"), check_vma=False
    )
```

```python
import functools

import jax
import jax.numpy as jnp
from jax import lax
from jax.experimental import pallas as pl
from jax.experimental.pallas import tpu as pltpu
from jax.sharding import PartitionSpec as P

MESH = pl.DeviceIdType.MESH
X, Y, H, L, C = 4, 4, 2, 8, 2
Z = H * L
B = X * H * C
LL = L // C
NC, FC = 4, 4


def dot_t(a, b):
    return lax.dot_general(a, b, (((1,), (1,)), ((), ())), preferred_element_type=jnp.float32)


def kernel(
    t_ref, w_ref, out_ref,
    zb, wc, rr, tb, t4, pf, pr, ys, yr, gb, po, xb, xr, ob, oc, acc,
    loc, s_z, r_z, s_x, s_m, r_m, r_w, s_p, r_p, s_y, r_y, s_g, s_h, r_g, s_q, r_q,
    s_l, r_l, s_o, s_c, s_r, r_o, s_t, r_t4, r_tp, s_u, r_t,
):
    dp, tn = lax.axis_index("dp"), lax.axis_index("tensor")
    y, l = lax.div(dp, L), lax.rem(dp, L)
    x, h, c = lax.div(tn, H * C), lax.rem(lax.div(tn, C), H), lax.rem(tn, C)
    z = h * L + l
    other = 1 - c
    rb, cb = w_ref.shape
    rows = t_ref.shape[0]
    cw = LL * cb
    r = rb // LL
    zr, fr, tr = rb // NC, r // FC, rows // 2

    def dev(ax, ay, az, ac):
        return (ay * L + lax.rem(az, L), (ax * H + lax.div(az, L)) * C + ac)

    def xs(k):
        return lax.rem(x + k, X)

    def yy(k):
        return lax.rem(y + k, Y)

    def zz(k):
        return lax.rem(z + k, Z)

    def send(src, dst, ssem, rsem, device):
        return pltpu.make_async_remote_copy(
            src_ref=src, dst_ref=dst, send_sem=ssem, recv_sem=rsem, device_id=device, device_id_type=MESH
        )

    def await_copy(ref, sem):
        pltpu.make_async_copy(ref, ref, sem).wait()

    def blk(ax, ah, ac):
        return (ax * H + ah) * C + ac

    def tblk(b):
        return tb.at[pl.ds(pl.multiple_of(b * rows, rows), rows), :]

    def thalf(b, i):
        return tb.at[pl.ds(pl.multiple_of(b * rows + i * tr, tr), tr), :]

    def part(ref, i):
        return ref.at[pl.ds(pl.multiple_of(i * r, r), r), :]

    mine, partner = blk(x, h, c), blk(x, 1 - h, c)
    loads = [pltpu.make_async_copy(w_ref.at[pl.ds(i * zr, zr), :], zb.at[z, i], loc.at[i]) for i in range(NC)]
    loads.append(pltpu.make_async_copy(t_ref, tblk(mine), loc.at[NC]))
    for load in loads:
        load.start()

    barrier = pltpu.get_barrier_semaphore()
    peers = [dev(x, y, zz(1), c), dev(x, y, zz(Z - 1), c), dev(x, y, z, other)]
    peers += [dev(xs(k), y, z, a) for k in (1, 2, 3) for a in (c, other)]
    peers += [dev(x, yy(k), z, a) for k in (1, Y - 1) for a in (c, other)] + [dev(x, yy(2), z, c)]
    for peer in peers:
        pl.semaphore_signal(barrier, inc=1, device_id=peer, device_id_type=MESH)
    pl.semaphore_wait(barrier, len(peers))
    for load in loads:
        load.wait()

    own_core, own_row = lax.div(l, LL), lax.rem(l, LL) * r
    own_chunk = lax.div(own_row, zr)

    def slot(b, i, k):
        return wc.at[b, pl.ds(i * zr, zr), pl.ds(pl.multiple_of(k * cb, cb), cb)]

    def up(q, i, sem=0):
        send(zb.at[q, i], zb.at[q, i], s_z.at[sem], r_z.at[q, i], dev(x, y, zz(1), c)).start()

    def down(q, i, sem=1):
        send(zb.at[q, i], zb.at[q, i], s_z.at[sem], r_z.at[q, i], dev(x, y, zz(Z - 1), c)).start()

    def spread(q, i):
        lq, hq = lax.rem(q, L), lax.div(q, L)
        to, k = lax.div(lq, LL), lax.rem(lq, LL)
        b = hq * C + c

        @pl.when((hq == h) & (own_core == c) & (own_chunk == i))
        def _():
            src = zb.at[q, i, pl.ds(pl.multiple_of(own_row - i * zr, r), r), :]
            dst = rr.at[pl.ds(pl.multiple_of(x * r, r), r), pl.ds(pl.multiple_of(k * cb, cb), cb)]
            for n in (2, 1, 3):
                send(src, dst, s_m, r_m.at[x, k], dev(xs(n), y, z, to)).start()

        @pl.when(to != c)
        def _():
            send(zb.at[q, i], slot(b, i, k), s_x, r_w.at[b, i, k], dev(x, y, z, other)).start()

        @pl.when(to == c)
        def _():
            pltpu.make_async_copy(zb.at[q, i], slot(b, i, k), r_w.at[b, i, k]).start()

    def t_spread(b):
        send(tblk(b), tblk(b), s_u.at[0], r_t.at[b], dev(xs(1), y, z, c)).start()
        send(tblk(b), tblk(b), s_u.at[1], r_t.at[b], dev(xs(X - 1), y, z, c)).start()

    def t_other(b):
        send(tblk(b), tblk(b), s_u.at[3], r_t.at[b], dev(x, y, z, other)).start()

    def t_pass(hq, a, b):
        near = blk(a, hq, c)
        await_copy(tblk(near), r_t.at[near])
        send(tblk(near), tblk(near), s_u.at[2], r_t.at[near], dev(b, y, z, c)).start()
        t_other(near)

    def t_turn(hq):
        @pl.when(hq == 0)
        def _():
            t_pass(0, xs(X - 1), xs(1))

        @pl.when(hq == 1)
        def _():
            t_pass(1, xs(1), xs(X - 1))
    for i in range(NC):
        up(z, i)
        down(z, i)
    for i in range(NC):
        spread(z, i)
    t_spread(mine)
    t_other(mine)

    def z_step(s, _):
        q, p = zz(Z - s), zz(s)
        for i in range(NC):
            await_copy(zb.at[q, i], r_z.at[q, i])
            up(q, i)
            await_copy(zb.at[p, i], r_z.at[p, i])
            down(p, i)
        for i in range(NC):
            spread(q, i)
            spread(p, i)
        return 0
    lax.fori_loop(1, Z // 2 - 1, z_step, 0)
    q, p = zz(Z // 2 + 1), zz(Z // 2 - 1)
    for i in range(NC):
        await_copy(zb.at[q, i], r_z.at[q, i])
        if i < NC // 2:
            up(q, i, 2)
        await_copy(zb.at[p, i], r_z.at[p, i])
        if i >= NC // 2:
            down(p, i, 3)
    for i in range(NC):
        spread(q, i)
        spread(p, i)

    quarter = Z // 4
    send(thalf(mine, 0), t4.at[0], s_t.at[0], r_t4.at[0], dev(x, y, zz(quarter), c)).start()
    send(thalf(mine, 1), t4.at[1], s_t.at[1], r_t4.at[1], dev(x, y, zz(Z - quarter), c)).start()
    t_turn(h)
    q = zz(Z // 2)
    for i in range(NC):
        await_copy(zb.at[q, i], r_z.at[q, i])
        spread(q, i)
    for b in range(H * C):
        for i in range(NC):
            for k in range(LL):
                await_copy(slot(b, i, k), r_w.at[b, i, k])
    for n in (1, 2, 3):
        for k in range(LL):
            await_copy(
                rr.at[pl.ds(pl.multiple_of(xs(n) * r, r), r), pl.ds(k * cb, cb)], r_m.at[xs(n), k]
            )

    half = H * C // C
    wr = wc[h * C + own_core, pl.ds(pl.multiple_of(own_row, r), r), :]
    rr[pl.ds(pl.multiple_of(x * r, r), r), :] = wr
    for i in range(half):
        b = other * half + i
        pf[b] = dot_t(rr[...], wc[b])
    half_copy = send(pf.at[pl.ds(other * half, half)], pr, s_p, r_p, dev(x, y, z, other))
    half_copy.start()
    for i in range(half):
        b = c * half + i
        pf[b] = dot_t(rr[...], wc[b])
    half_copy.wait_recv()
    for i in range(half):
        total = pf[c * half + i] + pr[i]
        pf[c * half + i] = total
        ys[i] = total.astype(jnp.bfloat16)

    def y_part(ref, k):
        return ref.at[:, pl.ds(pl.multiple_of(k * r, r), r), :]

    for k in (2, 1, Y - 1):
        send(y_part(ys, yy(k)), yr.at[k], s_y.at[k], r_y.at[k], dev(x, yy(k), z, c)).start()
    for k in (1, Y - 1, 2):
        await_copy(yr.at[k], r_y.at[k])
    my_rows = pl.ds(pl.multiple_of(y * r, r), r)
    for i, ahead, back in ((0, quarter, Z - quarter), (1, Z - quarter, quarter)):
        await_copy(t4.at[i], r_t4.at[i])
        home = blk(x, lax.div(zz(back), L), c)
        send(t4.at[i], thalf(home, i), s_t.at[2 + i], r_tp.at[i], dev(x, y, zz(ahead), c)).start()
    for i in range(half):
        total = pf[c * half + i, my_rows, :]
        for k in range(1, Y):
            total = total + yr[k, i].astype(jnp.float32)
        gb[c * half + i, my_rows, :] = total.astype(jnp.bfloat16)

    def g_at(a, k):
        return gb.at[pl.ds(a * half, half), pl.ds(pl.multiple_of(k * r, r), r), :]
    for k in (2, 1, Y - 1):
        send(g_at(c, y), g_at(c, y), s_g.at[k], r_g.at[c, y], dev(x, yy(k), z, c)).start()
    send(g_at(c, y), g_at(c, y), s_h.at[0], r_g.at[c, y], dev(x, y, z, other)).start()
    for k in (1, Y - 1, 2):
        await_copy(g_at(c, yy(k)), r_g.at[c, yy(k)])
        send(g_at(c, yy(k)), g_at(c, yy(k)), s_h.at[k], r_g.at[c, yy(k)], dev(x, y, z, other)).start()
    for k in range(Y):
        await_copy(g_at(other, yy(k)), r_g.at[other, yy(k)])

    total = jnp.dot(gb[0], wc[0], preferred_element_type=jnp.float32)
    for b in range(1, H * C):
        total = total + jnp.dot(gb[b], wc[b], preferred_element_type=jnp.float32)
    total = -0.5 * total
    po[...] = total
    xb[...] = total.astype(jnp.bfloat16)
    for n in (2, 1, 3):
        send(part(xb, xs(n)), xr.at[n], s_q.at[n], r_q.at[n], dev(xs(n), y, z, c)).start()
    for n in (1, 3, 2):
        await_copy(xr.at[n], r_q.at[n])
    total = 1.5 * wr.astype(jnp.float32) + po[pl.ds(pl.multiple_of(x * r, r), r), :]
    for n in (1, 2, 3):
        total = total + xr[n].astype(jnp.float32)
    for i in range(FC):
        ob[l, i] = total[i * fr:(i + 1) * fr].astype(jnp.bfloat16)

    def o_slot(a, k, i):
        return oc.at[a, pl.ds(pl.multiple_of(k * r + i * fr, fr), fr), :]

    def o_up(q, i):
        @pl.when(l < L - 1)
        def _():
            send(ob.at[q, i], ob.at[q, i], s_l.at[0, q], r_l.at[q, i], (dp + 1, tn)).start()

    def o_down(q, i):
        @pl.when(l > 0)
        def _():
            send(ob.at[q, i], ob.at[q, i], s_l.at[1, q], r_l.at[q, i], (dp - 1, tn)).start()

    def o_spread(q, i):
        to, k = lax.div(q, LL), lax.rem(q, LL)
        a = y * C + c
        dst, sem = o_slot(a, k, i), r_o.at[a, k, i]
        send(ob.at[q, i], dst, s_o.at[0], sem, dev(x, yy(1), z, to)).start()
        send(ob.at[q, i], dst, s_o.at[1], sem, dev(x, yy(Y - 1), z, to)).start()

        @pl.when(to != c)
        def _():
            send(ob.at[q, i], dst, s_c, sem, dev(x, y, z, other)).start()

        @pl.when(to == c)
        def _():
            pltpu.make_async_copy(ob.at[q, i], dst, sem).start()

    def o_relay(q):
        @pl.when(lax.div(q, LL) == c)
        def _():
            k = lax.rem(q, LL)
            for i in range(FC):
                for a, far in ((yy(Y - 1) * C, yy(1)), (yy(1) * C + 1, yy(Y - 1))):
                    await_copy(o_slot(a, k, i), r_o.at[a, k, i])
                    send(o_slot(a, k, i), o_slot(a, k, i), s_r, r_o.at[a, k, i], dev(x, far, z, c)).start()
    for i in range(FC):
        o_up(l, i)
        o_down(l, i)
    for i in range(FC):
        o_spread(l, i)

    def l_step(s, _):
        for i in range(FC):
            @pl.when(l - s >= 0)
            def _():
                await_copy(ob.at[l - s, i], r_l.at[l - s, i])
                o_up(l - s, i)

            @pl.when(l + s < L)
            def _():
                await_copy(ob.at[l + s, i], r_l.at[l + s, i])
                o_down(l + s, i)

        for i in range(FC):
            @pl.when(l - s >= 0)
            def _():
                o_spread(l - s, i)

            @pl.when(l + s < L)
            def _():
                o_spread(l + s, i)

        @pl.when(s == 2)
        def _():
            o_relay(l)

        @pl.when((s > 2) & (l - s + 2 >= 0))
        def _():
            o_relay(l - s + 2)

        @pl.when((s > 2) & (l + s - 2 < L))
        def _():
            o_relay(l + s - 2)

        @pl.when(s == 1)
        def _():
            await_copy(thalf(partner, 0), r_tp.at[0])
            await_copy(thalf(partner, 1), r_tp.at[1])
            t_spread(partner)
            t_other(partner)

        @pl.when(s == 4)
        def _():
            t_turn(1 - h)

        return 0
    lax.fori_loop(1, L, l_step, 0)
    for s in (L - 2, L - 1):
        @pl.when(l - s >= 0)
        def _():
            o_relay(l - s)

        @pl.when(l + s < L)
        def _():
            o_relay(l + s)
    for hq, a in ((1, xs(X - 1)), (0, xs(1)), (0, xs(2)), (1, xs(2))):
        b = blk(a, hq, c)
        await_copy(tblk(b), r_t.at[b])
        t_other(b)
    for k in range(X):
        for hq in range(H):
            b = blk(xs(k), hq, other)
            await_copy(tblk(b), r_t.at[b])

    acc[...] = jnp.zeros_like(acc)

    def take(a):
        for k in range(LL):
            for i in range(FC):
                await_copy(o_slot(a, k, i), r_o.at[a, k, i])

    def project(i, first):
        a = lax.rem(first + i, Y * C)
        acc[...] += dot_t(tb[:, pl.ds(pl.multiple_of(a * cw, cw), cw)], oc[a])
        return first
    for a in (y * C, y * C + 1, yy(Y - 1) * C + 1, yy(1) * C):
        take(a)
    lax.fori_loop(0, 3 * C, project, yy(Y - 1) * C)
    take(yy(2) * C)
    take(yy(2) * C + 1)
    lax.fori_loop(0, C, project, yy(2) * C)
    out_ref[...] = acc[...].astype(jnp.bfloat16)

    def sent(ref, sem):
        pltpu.make_async_copy(ref, ref, sem).wait()
    for n in range(2):
        sent(zb.at[pl.ds(0, Z // 2 - 1)], s_z.at[n])
        sent(zb.at[0, pl.ds(0, NC // 2)], s_z.at[2 + n])
    sent(zb.at[pl.ds(0, Z // 2)], s_x)

    @pl.when(own_core == c)
    def _():
        sent(zb.at[pl.ds(0, L * 3 // LL)], s_m)

    half_copy.wait_send()
    for k in range(1, Y):
        sent(yr.at[k], s_y.at[k])
        sent(yr.at[k], s_g.at[k])
        sent(xr.at[k], s_q.at[k])
    for k in range(Y):
        sent(yr.at[0], s_h.at[k])
    for k in range(4):
        sent(t4.at[0], s_t.at[k])
    two, eight = tb.at[pl.ds(0, H * rows), :], tb.at[pl.ds(0, X * H * rows), :]
    sent(two, s_u.at[0])
    sent(two, s_u.at[1])
    sent(two, s_u.at[2])
    sent(eight, s_u.at[3])
    sent(ob, s_o.at[0])
    sent(ob, s_o.at[1])
    sent(ob.at[pl.ds(0, L // 2)], s_c)
    sent(ob, s_r)

    def line(q, _):
        @pl.when((l < L - 1) & (q <= l))
        def _():
            sent(ob.at[q], s_l.at[0, q])

        @pl.when((l > 0) & (q >= l))
        def _():
            sent(ob.at[q], s_l.at[1, q])

        return 0

    lax.fori_loop(0, L, line, 0)


def on_device(tokens, weight):
    rows, d = tokens.shape
    rb, cb = weight.shape
    cw, r, half = LL * cb, rb // LL, H
    dma = pltpu.SemaphoreType.DMA
    bf, f32 = jnp.bfloat16, jnp.float32
    return pl.pallas_call(
        kernel,
        out_shape=jax.ShapeDtypeStruct((B * rows, rb), bf),
        in_specs=[pl.BlockSpec(memory_space=pl.ANY)] * 2,
        out_specs=pl.BlockSpec(memory_space=pltpu.VMEM),
        scratch_shapes=[
            pltpu.VMEM((Z, NC, rb // NC, cb), bf),
            pltpu.VMEM((H * C, rb, cw), bf),
            pltpu.VMEM((X * r, cw), bf),
            pltpu.VMEM((B * rows, d), bf),
            pltpu.VMEM((2, rows // 2, d), bf),
            pltpu.VMEM((H * C, X * r, rb), f32),
            pltpu.VMEM((half, X * r, rb), f32),
            pltpu.VMEM((half, X * r, rb), bf),
            pltpu.VMEM((Y, half, r, rb), bf),
            pltpu.VMEM((H * C, X * r, rb), bf),
            pltpu.VMEM((X * r, cw), f32),
            pltpu.VMEM((X * r, cw), bf),
            pltpu.VMEM((X, r, cw), bf),
            pltpu.VMEM((L, FC, r // FC, cw), bf),
            pltpu.VMEM((Y * C, rb, cw), bf),
            pltpu.VMEM((B * rows, rb), f32),
            dma((NC + 1,)),
            dma((4,)), dma((Z, NC)), dma, dma, dma((X, LL)), dma((H * C, NC, LL)),
            dma, dma, dma((Y,)), dma((Y,)), dma((Y,)), dma((Y,)), dma((C, Y)), dma((X,)), dma((X,)),
            dma((2, L)), dma((L, FC)), dma((2,)), dma, dma, dma((Y * C, LL, FC)),
            dma((4,)), dma((2,)), dma((2,)), dma((4,)), dma((B,)),
        ],
        compiler_params=pltpu.CompilerParams(
            collective_id=0, has_side_effects=True, vmem_limit_bytes=64_000_000
        ),
        name="bjorck",
    )(tokens, weight)


def solution(mesh):
    placed = (P(("dp", "tensor"), None), P("tensor", "dp"))
    return jax.shard_map(
        on_device, mesh=mesh, in_specs=placed, out_specs=P("dp", "tensor"), check_vma=False
    )
```

```python
import functools

import jax
import jax.numpy as jnp
from jax import lax
from jax.experimental import pallas as pl
from jax.experimental.pallas import tpu as pltpu
from jax.sharding import PartitionSpec as P

MESH = pl.DeviceIdType.MESH
X, Y, H, L, C = 4, 4, 2, 8, 2
Z = H * L
B = X * H * C
LL = L // C
NC, FC = 2, 2


def dot_t(a, b):
    return lax.dot_general(a, b, (((1,), (1,)), ((), ())), preferred_element_type=jnp.float32)


def kernel(
    t_ref, w_ref, out_ref,
    zb, wc, rr, tb, pf, pr, ys, yr, gb, po, xb, xr, ob, oc, acc,
    loc, s_z, r_z, s_x, s_m, r_m, r_w, s_p, r_p, s_y, r_y, s_g, s_h, r_g, s_q, r_q,
    s_l, r_l, s_o, s_c, r_o, s_t, s_u, r_t,
):
    dp, tn = lax.axis_index("dp"), lax.axis_index("tensor")
    y, l = lax.div(dp, L), lax.rem(dp, L)
    x, h, c = lax.div(tn, H * C), lax.rem(lax.div(tn, C), H), lax.rem(tn, C)
    z = h * L + l
    other = 1 - c
    rb, cb = w_ref.shape
    rows = t_ref.shape[0]
    cw = LL * cb
    r = rb // LL
    zr, fr = rb // NC, r // FC

    def dev(ax, ay, az, ac):
        return (ay * L + lax.rem(az, L), (ax * H + lax.div(az, L)) * C + ac)

    def xs(k):
        return lax.rem(x + k, X)

    def yy(k):
        return lax.rem(y + k, Y)

    def zz(k):
        return lax.rem(z + k, Z)

    def send(src, dst, ssem, rsem, device):
        return pltpu.make_async_remote_copy(
            src_ref=src, dst_ref=dst, send_sem=ssem, recv_sem=rsem, device_id=device, device_id_type=MESH
        )

    def await_copy(ref, sem):
        pltpu.make_async_copy(ref, ref, sem).wait()

    def blk(ax, ah, ac):
        return (ax * H + ah) * C + ac

    def tblk(b):
        return tb.at[pl.ds(pl.multiple_of(b * rows, rows), rows), :]

    def part(ref, i):
        return ref.at[pl.ds(pl.multiple_of(i * r, r), r), :]

    mine, partner = blk(x, h, c), blk(x, 1 - h, c)
    loads = [pltpu.make_async_copy(w_ref.at[pl.ds(i * zr, zr), :], zb.at[z, i], loc.at[i]) for i in range(NC)]
    loads.append(pltpu.make_async_copy(t_ref, tblk(mine), loc.at[NC]))
    for load in loads:
        load.start()

    barrier = pltpu.get_barrier_semaphore()
    peers = [dev(x, y, zz(k), c) for k in (1, 2, 3, Z - 3, Z - 2, Z - 1)] + [dev(x, y, z, other)]
    peers += [dev(xs(k), y, z, a) for k in (1, 2, 3) for a in (c, other)]
    peers += [dev(x, yy(k), z, a) for k in (1, 2, 3) for a in (c, other)]
    for peer in peers:
        pl.semaphore_signal(barrier, inc=1, device_id=peer, device_id_type=MESH)
    pl.semaphore_wait(barrier, len(peers))
    for load in loads:
        load.wait()

    own_core, own_row = lax.div(l, LL), lax.rem(l, LL) * r
    own_chunk = lax.div(own_row, zr)

    def slot(b, i, k):
        return wc.at[b, pl.ds(i * zr, zr), pl.ds(pl.multiple_of(k * cb, cb), cb)]

    def go(q, i, k):
        send(zb.at[q, i], zb.at[q, i], s_z, r_z.at[q, i], dev(x, y, zz(k % Z), c)).start()

    def spread(q, i):
        lq, hq = lax.rem(q, L), lax.div(q, L)
        to, k = lax.div(lq, LL), lax.rem(lq, LL)
        b = hq * C + c

        @pl.when((hq == h) & (own_core == c) & (own_chunk == i))
        def _():
            src = zb.at[q, i, pl.ds(pl.multiple_of(own_row - i * zr, r), r), :]
            dst = rr.at[pl.ds(pl.multiple_of(x * r, r), r), pl.ds(pl.multiple_of(k * cb, cb), cb)]
            for n in (2, 1, 3):
                send(src, dst, s_m, r_m.at[x, k], dev(xs(n), y, z, to)).start()

        @pl.when(to != c)
        def _():
            send(zb.at[q, i], slot(b, i, k), s_x, r_w.at[b, i, k], dev(x, y, z, other)).start()

        @pl.when(to == c)
        def _():
            pltpu.make_async_copy(zb.at[q, i], slot(b, i, k), r_w.at[b, i, k]).start()

    def t_spread(b):
        for n in (2, 1, 3):
            send(tblk(b), tblk(b), s_u.at[n], r_t.at[b], dev(xs(n), y, z, c)).start()

    def t_other(b):
        send(tblk(b), tblk(b), s_u.at[0], r_t.at[b], dev(x, y, z, other)).start()

    def t_arrived(b):
        await_copy(tblk(b), r_t.at[b])
        t_other(b)
    for k in (3, 2, 1):
        for i in range(NC):
            go(z, i, k)
            go(z, i, -k)
    for i in range(NC):
        spread(z, i)
    t_spread(mine)
    t_other(mine)

    for n in range(1, Z // 2):
        for i in range(NC):
            for way in (1, -1):
                q = zz((-way * n) % Z)
                await_copy(zb.at[q, i], r_z.at[q, i])
                if n == 3:
                    for k in (3, 2, 1):
                        go(q, i, way * k)
                if n == 6:
                    if (way == 1) == (i < NC // 2):
                        go(q, i, way * 2)
                    go(q, i, way)
        for i in range(NC):
            for way in (1, -1):
                spread(zz((-way * n) % Z), i)
    q = zz(Z // 2)
    for i in range(NC):
        await_copy(zb.at[q, i], r_z.at[q, i])
        spread(q, i)
    send(tblk(mine), tblk(mine), s_t, r_t.at[mine], dev(x, y, zz(Z // 2), c)).start()
    for b in range(H * C):
        for i in range(NC):
            for k in range(LL):
                await_copy(slot(b, i, k), r_w.at[b, i, k])
    for n in (1, 2, 3):
        for k in range(LL):
            await_copy(
                rr.at[pl.ds(pl.multiple_of(xs(n) * r, r), r), pl.ds(k * cb, cb)], r_m.at[xs(n), k]
            )

    half = H * C // C
    wr = wc[h * C + own_core, pl.ds(pl.multiple_of(own_row, r), r), :]
    rr[pl.ds(pl.multiple_of(x * r, r), r), :] = wr
    for i in range(half):
        b = other * half + i
        pf[b] = dot_t(rr[...], wc[b])
    half_copy = send(pf.at[pl.ds(other * half, half)], pr, s_p, r_p, dev(x, y, z, other))
    half_copy.start()
    for i in range(half):
        b = c * half + i
        pf[b] = dot_t(rr[...], wc[b])
    half_copy.wait_recv()
    for i in range(half):
        total = pf[c * half + i] + pr[i]
        pf[c * half + i] = total
        ys[i] = total.astype(jnp.bfloat16)

    def y_part(ref, k):
        return ref.at[:, pl.ds(pl.multiple_of(k * r, r), r), :]

    for k in (2, 1, Y - 1):
        send(y_part(ys, yy(k)), yr.at[k], s_y.at[k], r_y.at[k], dev(x, yy(k), z, c)).start()
    for k in (1, Y - 1, 2):
        await_copy(yr.at[k], r_y.at[k])
    my_rows = pl.ds(pl.multiple_of(y * r, r), r)
    for n in (1, 3, 2):
        t_arrived(blk(xs(n), h, c))
    for i in range(half):
        total = pf[c * half + i, my_rows, :]
        for k in range(1, Y):
            total = total + yr[k, i].astype(jnp.float32)
        gb[c * half + i, my_rows, :] = total.astype(jnp.bfloat16)

    def g_at(a, k):
        return gb.at[pl.ds(a * half, half), pl.ds(pl.multiple_of(k * r, r), r), :]
    for k in (2, 1, Y - 1):
        send(g_at(c, y), g_at(c, y), s_g.at[k], r_g.at[c, y], dev(x, yy(k), z, c)).start()
    send(g_at(c, y), g_at(c, y), s_h.at[0], r_g.at[c, y], dev(x, y, z, other)).start()
    for k in (1, Y - 1, 2):
        await_copy(g_at(c, yy(k)), r_g.at[c, yy(k)])
        send(g_at(c, yy(k)), g_at(c, yy(k)), s_h.at[k], r_g.at[c, yy(k)], dev(x, y, z, other)).start()
    for k in range(Y):
        await_copy(g_at(other, yy(k)), r_g.at[other, yy(k)])

    total = jnp.dot(gb[0], wc[0], preferred_element_type=jnp.float32)
    for b in range(1, H * C):
        total = total + jnp.dot(gb[b], wc[b], preferred_element_type=jnp.float32)
    total = -0.5 * total
    po[...] = total
    xb[...] = total.astype(jnp.bfloat16)
    for n in (2, 1, 3):
        send(part(xb, xs(n)), xr.at[n], s_q.at[n], r_q.at[n], dev(xs(n), y, z, c)).start()
    for n in (1, 3, 2):
        await_copy(xr.at[n], r_q.at[n])
    total = 1.5 * wr.astype(jnp.float32) + po[pl.ds(pl.multiple_of(x * r, r), r), :]
    for n in (1, 2, 3):
        total = total + xr[n].astype(jnp.float32)
    for i in range(FC):
        ob[l, i] = total[i * fr:(i + 1) * fr].astype(jnp.bfloat16)

    def o_slot(a, k, i):
        return oc.at[a, pl.ds(pl.multiple_of(k * r + i * fr, fr), fr), :]

    def along(q, i, k, n):
        @pl.when((l + k >= 0) & (l + k < L))
        def _():
            send(ob.at[q, i], ob.at[q, i], s_l.at[n], r_l.at[q, i], (dp + k, tn)).start()

    def o_spread(q, i):
        to, k = lax.div(q, LL), lax.rem(q, LL)
        a = y * C + c
        dst, sem = o_slot(a, k, i), r_o.at[a, k, i]
        for n in (2, 1, 3):
            send(ob.at[q, i], dst, s_o.at[n], sem, dev(x, yy(n), z, to)).start()

        @pl.when(to != c)
        def _():
            send(ob.at[q, i], dst, s_c, sem, dev(x, y, z, other)).start()

        @pl.when(to == c)
        def _():
            pltpu.make_async_copy(ob.at[q, i], dst, sem).start()

    half_line = L // 2
    ways = [way * k for k in range(half_line, 0, -1) for way in (1, -1)]
    for i in range(FC):
        for n, k in enumerate(ways):
            along(l, i, k, n)
    for i in range(FC):
        o_spread(l, i)

    t_arrived(partner)
    t_spread(partner)
    for n in range(1, L):
        for i in range(FC):
            for way in (1, -1):
                q = l - way * n

                @pl.when((q >= 0) & (q < L))
                def _():
                    await_copy(ob.at[q, i], r_l.at[q, i])
                    if n == half_line:
                        for k in range(half_line - 1, 0, -1):
                            along(q, i, way * k, len(ways) + ways.index(way * k))
                    o_spread(q, i)
    for n in (1, 3, 2):
        t_arrived(blk(xs(n), 1 - h, c))
    for k in range(X):
        for hq in range(H):
            b = blk(xs(k), hq, other)
            await_copy(tblk(b), r_t.at[b])

    acc[...] = jnp.zeros_like(acc)

    def take(a):
        for k in range(LL):
            for i in range(FC):
                await_copy(o_slot(a, k, i), r_o.at[a, k, i])

    def project(i, first):
        a = lax.rem(first + i, Y * C)
        acc[...] += dot_t(tb[:, pl.ds(pl.multiple_of(a * cw, cw), cw)], oc[a])
        return first
    for k in (0, 1, Y - 1):
        take(yy(k) * C)
        take(yy(k) * C + 1)
    lax.fori_loop(0, 3 * C, project, yy(Y - 1) * C)
    take(yy(2) * C)
    take(yy(2) * C + 1)
    lax.fori_loop(0, C, project, yy(2) * C)
    out_ref[...] = acc[...].astype(jnp.bfloat16)

    def sent(ref, sem):
        pltpu.make_async_copy(ref, ref, sem).wait()
    sent(zb.at[pl.ds(0, Z - 1)], s_z)
    sent(zb.at[pl.ds(0, Z // 2)], s_x)

    @pl.when(own_core == c)
    def _():
        sent(zb.at[pl.ds(0, L * 3 // LL)], s_m)

    half_copy.wait_send()
    for k in range(1, Y):
        sent(yr.at[k], s_y.at[k])
        sent(yr.at[k], s_g.at[k])
        sent(xr.at[k], s_q.at[k])
    for k in range(Y):
        sent(yr.at[0], s_h.at[k])
    sent(tblk(mine), s_t)
    for n in (1, 2, 3):
        sent(tb.at[pl.ds(0, H * rows), :], s_u.at[n])
        sent(ob, s_o.at[n])
    sent(tb.at[pl.ds(0, X * H * rows), :], s_u.at[0])
    sent(ob.at[pl.ds(0, L // 2)], s_c)
    for n, k in enumerate(ways):
        @pl.when((l + k >= 0) & (l + k < L))
        def _():
            sent(ob.at[0], s_l.at[n])

        if abs(k) < half_line:
            far = l + k - (half_line if k > 0 else -half_line) - k

            @pl.when((l + k >= 0) & (l + k < L) & (far >= 0) & (far < L))
            def _():
                sent(ob.at[0], s_l.at[len(ways) + n])


def on_device(tokens, weight):
    rows, d = tokens.shape
    rb, cb = weight.shape
    cw, r, half = LL * cb, rb // LL, H
    dma = pltpu.SemaphoreType.DMA
    bf, f32 = jnp.bfloat16, jnp.float32
    return pl.pallas_call(
        kernel,
        out_shape=jax.ShapeDtypeStruct((B * rows, rb), bf),
        in_specs=[pl.BlockSpec(memory_space=pl.ANY)] * 2,
        out_specs=pl.BlockSpec(memory_space=pltpu.VMEM),
        scratch_shapes=[
            pltpu.VMEM((Z, NC, rb // NC, cb), bf),
            pltpu.VMEM((H * C, rb, cw), bf),
            pltpu.VMEM((X * r, cw), bf),
            pltpu.VMEM((B * rows, d), bf),
            pltpu.VMEM((H * C, X * r, rb), f32),
            pltpu.VMEM((half, X * r, rb), f32),
            pltpu.VMEM((half, X * r, rb), bf),
            pltpu.VMEM((Y, half, r, rb), bf),
            pltpu.VMEM((H * C, X * r, rb), bf),
            pltpu.VMEM((X * r, cw), f32),
            pltpu.VMEM((X * r, cw), bf),
            pltpu.VMEM((X, r, cw), bf),
            pltpu.VMEM((L, FC, r // FC, cw), bf),
            pltpu.VMEM((Y * C, rb, cw), bf),
            pltpu.VMEM((B * rows, rb), f32),
            dma((NC + 1,)),
            dma, dma((Z, NC)), dma, dma, dma((X, LL)), dma((H * C, NC, LL)),
            dma, dma, dma((Y,)), dma((Y,)), dma((Y,)), dma((Y,)), dma((C, Y)), dma((X,)), dma((X,)),
            dma((2 * L,)), dma((L, FC)), dma((Y,)), dma, dma((Y * C, LL, FC)),
            dma, dma((X,)), dma((B,)),
        ],
        compiler_params=pltpu.CompilerParams(
            collective_id=0, has_side_effects=True, vmem_limit_bytes=64_000_000
        ),
        name="bjorck",
    )(tokens, weight)


def solution(mesh):
    placed = (P(("dp", "tensor"), None), P("tensor", "dp"))
    return jax.shard_map(
        on_device, mesh=mesh, in_specs=placed, out_specs=P("dp", "tensor"), check_vma=False
    )
```

```python
import functools

import jax
import jax.numpy as jnp
from jax import lax
from jax.experimental import pallas as pl
from jax.experimental.pallas import tpu as pltpu
from jax.sharding import PartitionSpec as P

MESH = pl.DeviceIdType.MESH
X, Y, H, L, C = 4, 4, 2, 8, 2
Z = H * L
B = X * H * C
LL = L // C
NC, FC = 2, 4


def dot_t(a, b):
    return lax.dot_general(a, b, (((1,), (1,)), ((), ())), preferred_element_type=jnp.float32)


def kernel(
    t_ref, w_ref, out_ref,
    zb, wc, rr, tb, t4, pf, pr, ys, yr, gb, po, xb, xr, ob, oc, acc,
    loc, s_z, r_z, s_x, s_m, r_m, r_w, s_p, r_p, s_y, r_y, s_g, s_h, r_g, s_q, r_q,
    s_l, r_l, s_o, s_c, s_r, r_o, s_t, r_t4, r_tp, s_u, r_t,
):
    dp, tn = lax.axis_index("dp"), lax.axis_index("tensor")
    y, l = lax.div(dp, L), lax.rem(dp, L)
    x, h, c = lax.div(tn, H * C), lax.rem(lax.div(tn, C), H), lax.rem(tn, C)
    z = h * L + l
    other = 1 - c
    rb, cb = w_ref.shape
    rows = t_ref.shape[0]
    cw = LL * cb
    r = rb // LL
    zr, fr, tr = rb // NC, r // FC, rows // 2

    def dev(ax, ay, az, ac):
        return (ay * L + lax.rem(az, L), (ax * H + lax.div(az, L)) * C + ac)

    def xs(k):
        return lax.rem(x + k, X)

    def yy(k):
        return lax.rem(y + k, Y)

    def zz(k):
        return lax.rem(z + k, Z)

    def send(src, dst, ssem, rsem, device):
        return pltpu.make_async_remote_copy(
            src_ref=src, dst_ref=dst, send_sem=ssem, recv_sem=rsem, device_id=device, device_id_type=MESH
        )

    def await_copy(ref, sem):
        pltpu.make_async_copy(ref, ref, sem).wait()

    def blk(ax, ah, ac):
        return (ax * H + ah) * C + ac

    def tblk(b):
        return tb.at[pl.ds(pl.multiple_of(b * rows, rows), rows), :]

    def thalf(b, i):
        return tb.at[pl.ds(pl.multiple_of(b * rows + i * tr, tr), tr), :]

    def part(ref, i):
        return ref.at[pl.ds(pl.multiple_of(i * r, r), r), :]

    mine, partner = blk(x, h, c), blk(x, 1 - h, c)
    loads = [pltpu.make_async_copy(w_ref.at[pl.ds(i * zr, zr), :], zb.at[z, i], loc.at[i]) for i in range(NC)]
    loads.append(pltpu.make_async_copy(t_ref, tblk(mine), loc.at[NC]))
    for load in loads:
        load.start()

    barrier = pltpu.get_barrier_semaphore()
    peers = [dev(x, y, zz(k), c) for k in (1, 2, Z - 2, Z - 1)] + [dev(x, y, z, other)]
    peers += [dev(xs(k), y, z, a) for k in (1, 2, 3) for a in (c, other)]
    peers += [dev(x, yy(k), z, a) for k in (1, 2, 3) for a in (c, other)]
    for peer in peers:
        pl.semaphore_signal(barrier, inc=1, device_id=peer, device_id_type=MESH)
    pl.semaphore_wait(barrier, len(peers))
    for load in loads:
        load.wait()

    own_core, own_row = lax.div(l, LL), lax.rem(l, LL) * r
    own_chunk = lax.div(own_row, zr)

    def slot(b, i, k):
        return wc.at[b, pl.ds(i * zr, zr), pl.ds(pl.multiple_of(k * cb, cb), cb)]

    def go(q, i, k):
        send(zb.at[q, i], zb.at[q, i], s_z, r_z.at[q, i], dev(x, y, zz(k % Z), c)).start()

    def spread(q, i):
        lq, hq = lax.rem(q, L), lax.div(q, L)
        to, k = lax.div(lq, LL), lax.rem(lq, LL)
        b = hq * C + c

        @pl.when((hq == h) & (own_core == c) & (own_chunk == i))
        def _():
            src = zb.at[q, i, pl.ds(pl.multiple_of(own_row - i * zr, r), r), :]
            dst = rr.at[pl.ds(pl.multiple_of(x * r, r), r), pl.ds(pl.multiple_of(k * cb, cb), cb)]
            for n in (2, 1, 3):
                send(src, dst, s_m, r_m.at[x, k], dev(xs(n), y, z, to)).start()

        @pl.when(to != c)
        def _():
            send(zb.at[q, i], slot(b, i, k), s_x, r_w.at[b, i, k], dev(x, y, z, other)).start()

        @pl.when(to == c)
        def _():
            pltpu.make_async_copy(zb.at[q, i], slot(b, i, k), r_w.at[b, i, k]).start()

    def t_spread(b, to):
        for n in to:
            send(tblk(b), tblk(b), s_u.at[n], r_t.at[b], dev(xs(n), y, z, c)).start()

    def t_other(b):
        send(tblk(b), tblk(b), s_u.at[0], r_t.at[b], dev(x, y, z, other)).start()

    def t_arrived(b):
        await_copy(tblk(b), r_t.at[b])
        t_other(b)
    for k in (2, 1):
        for i in range(NC):
            go(z, i, k)
            go(z, i, -k)
    for i in range(NC):
        spread(z, i)
    t_spread(mine, (2, 1, 3))
    t_other(mine)

    for n in range(1, Z // 2):
        for i in range(NC):
            for way in (1, -1):
                q = zz((-way * n) % Z)
                await_copy(zb.at[q, i], r_z.at[q, i])
                if n in (2, 4):
                    for k in (2, 1):
                        go(q, i, way * k)
                if n == 6:
                    if (way == 1) == (i < NC // 2):
                        go(q, i, way * 2)
                    go(q, i, way)
        for i in range(NC):
            for way in (1, -1):
                spread(zz((-way * n) % Z), i)
    quarter = Z // 4
    send(thalf(mine, 0), t4.at[0], s_t.at[0], r_t4.at[0], dev(x, y, zz(quarter), c)).start()
    send(thalf(mine, 1), t4.at[1], s_t.at[1], r_t4.at[1], dev(x, y, zz(Z - quarter), c)).start()
    q = zz(Z // 2)
    for i in range(NC):
        await_copy(zb.at[q, i], r_z.at[q, i])
        spread(q, i)
    for b in range(H * C):
        for i in range(NC):
            for k in range(LL):
                await_copy(slot(b, i, k), r_w.at[b, i, k])
    for n in (1, 2, 3):
        for k in range(LL):
            await_copy(
                rr.at[pl.ds(pl.multiple_of(xs(n) * r, r), r), pl.ds(k * cb, cb)], r_m.at[xs(n), k]
            )

    half = H * C // C
    wr = wc[h * C + own_core, pl.ds(pl.multiple_of(own_row, r), r), :]
    rr[pl.ds(pl.multiple_of(x * r, r), r), :] = wr
    for i in range(half):
        b = other * half + i
        pf[b] = dot_t(rr[...], wc[b])
    half_copy = send(pf.at[pl.ds(other * half, half)], pr, s_p, r_p, dev(x, y, z, other))
    half_copy.start()
    for i in range(half):
        b = c * half + i
        pf[b] = dot_t(rr[...], wc[b])
    half_copy.wait_recv()
    for i in range(half):
        total = pf[c * half + i] + pr[i]
        pf[c * half + i] = total
        ys[i] = total.astype(jnp.bfloat16)

    def y_part(ref, k):
        return ref.at[:, pl.ds(pl.multiple_of(k * r, r), r), :]

    for k in (2, 1, Y - 1):
        send(y_part(ys, yy(k)), yr.at[k], s_y.at[k], r_y.at[k], dev(x, yy(k), z, c)).start()
    for k in (1, Y - 1, 2):
        await_copy(yr.at[k], r_y.at[k])
    my_rows = pl.ds(pl.multiple_of(y * r, r), r)
    for n in (1, 3, 2):
        t_arrived(blk(xs(n), h, c))
    for i in range(half):
        total = pf[c * half + i, my_rows, :]
        for k in range(1, Y):
            total = total + yr[k, i].astype(jnp.float32)
        gb[c * half + i, my_rows, :] = total.astype(jnp.bfloat16)

    def g_at(a, k):
        return gb.at[pl.ds(a * half, half), pl.ds(pl.multiple_of(k * r, r), r), :]
    for k in (2, 1, Y - 1):
        send(g_at(c, y), g_at(c, y), s_g.at[k], r_g.at[c, y], dev(x, yy(k), z, c)).start()
    send(g_at(c, y), g_at(c, y), s_h.at[0], r_g.at[c, y], dev(x, y, z, other)).start()
    for k in (1, Y - 1, 2):
        await_copy(g_at(c, yy(k)), r_g.at[c, yy(k)])
        send(g_at(c, yy(k)), g_at(c, yy(k)), s_h.at[k], r_g.at[c, yy(k)], dev(x, y, z, other)).start()
    for i, ahead, back in ((0, quarter, Z - quarter), (1, Z - quarter, quarter)):
        await_copy(t4.at[i], r_t4.at[i])
        home = blk(x, lax.div(zz(back), L), c)
        send(t4.at[i], thalf(home, i), s_t.at[2 + i], r_tp.at[i], dev(x, y, zz(ahead), c)).start()
    for k in range(Y):
        await_copy(g_at(other, yy(k)), r_g.at[other, yy(k)])

    total = jnp.dot(gb[0], wc[0], preferred_element_type=jnp.float32)
    for b in range(1, H * C):
        total = total + jnp.dot(gb[b], wc[b], preferred_element_type=jnp.float32)
    total = -0.5 * total
    po[...] = total
    xb[...] = total.astype(jnp.bfloat16)
    for n in (2, 1, 3):
        send(part(xb, xs(n)), xr.at[n], s_q.at[n], r_q.at[n], dev(xs(n), y, z, c)).start()
    for n in (1, 3, 2):
        await_copy(xr.at[n], r_q.at[n])
    total = 1.5 * wr.astype(jnp.float32) + po[pl.ds(pl.multiple_of(x * r, r), r), :]
    for n in (1, 2, 3):
        total = total + xr[n].astype(jnp.float32)
    for i in range(FC):
        ob[l, i] = total[i * fr:(i + 1) * fr].astype(jnp.bfloat16)

    def o_slot(a, k, i):
        return oc.at[a, pl.ds(pl.multiple_of(k * r + i * fr, fr), fr), :]

    def o_up(q, i):
        @pl.when(l < L - 1)
        def _():
            send(ob.at[q, i], ob.at[q, i], s_l.at[0, q], r_l.at[q, i], (dp + 1, tn)).start()

    def o_down(q, i):
        @pl.when(l > 0)
        def _():
            send(ob.at[q, i], ob.at[q, i], s_l.at[1, q], r_l.at[q, i], (dp - 1, tn)).start()

    def o_spread(q, i):
        to, k = lax.div(q, LL), lax.rem(q, LL)
        a = y * C + c
        dst, sem = o_slot(a, k, i), r_o.at[a, k, i]
        send(ob.at[q, i], dst, s_o.at[0], sem, dev(x, yy(1), z, to)).start()
        send(ob.at[q, i], dst, s_o.at[1], sem, dev(x, yy(Y - 1), z, to)).start()

        @pl.when(to != c)
        def _():
            send(ob.at[q, i], dst, s_c, sem, dev(x, y, z, other)).start()

        @pl.when(to == c)
        def _():
            pltpu.make_async_copy(ob.at[q, i], dst, sem).start()

    def o_relay(q):
        @pl.when(lax.div(q, LL) == c)
        def _():
            k = lax.rem(q, LL)
            for i in range(FC):
                for a, far in ((yy(Y - 1) * C, yy(1)), (yy(1) * C + 1, yy(Y - 1))):
                    await_copy(o_slot(a, k, i), r_o.at[a, k, i])
                    send(o_slot(a, k, i), o_slot(a, k, i), s_r, r_o.at[a, k, i], dev(x, far, z, c)).start()
    for i in range(FC):
        o_up(l, i)
        o_down(l, i)
    for i in range(FC):
        o_spread(l, i)

    def l_step(s, _):
        for i in range(FC):
            @pl.when(l - s >= 0)
            def _():
                await_copy(ob.at[l - s, i], r_l.at[l - s, i])
                o_up(l - s, i)

            @pl.when(l + s < L)
            def _():
                await_copy(ob.at[l + s, i], r_l.at[l + s, i])
                o_down(l + s, i)

        for i in range(FC):
            @pl.when(l - s >= 0)
            def _():
                o_spread(l - s, i)

            @pl.when(l + s < L)
            def _():
                o_spread(l + s, i)

        @pl.when(s == 2)
        def _():
            o_relay(l)

        @pl.when((s > 2) & (l - s + 2 >= 0))
        def _():
            o_relay(l - s + 2)

        @pl.when((s > 2) & (l + s - 2 < L))
        def _():
            o_relay(l + s - 2)

        @pl.when(s == 2)
        def _():
            await_copy(thalf(partner, 0), r_tp.at[0])
            await_copy(thalf(partner, 1), r_tp.at[1])
            t_spread(partner, (1, 3))
            t_other(partner)

        @pl.when(s == 5)
        def _():
            for i, near, far in ((0, xs(3), xs(1)), (1, xs(1), xs(3))):
                b = blk(near, 1 - h, c)
                await_copy(tblk(b), r_t.at[b])
                send(thalf(b, i), thalf(b, i), s_u.at[X + i], r_t.at[b], dev(far, y, z, c)).start()
                t_other(b)

        return 0
    lax.fori_loop(1, L, l_step, 0)
    for s in (L - 2, L - 1):
        @pl.when(l - s >= 0)
        def _():
            o_relay(l - s)

        @pl.when(l + s < L)
        def _():
            o_relay(l + s)
    t_arrived(blk(xs(2), 1 - h, c))
    for k in range(X):
        for hq in range(H):
            b = blk(xs(k), hq, other)
            await_copy(tblk(b), r_t.at[b])

    acc[...] = jnp.zeros_like(acc)

    def take(a):
        for k in range(LL):
            for i in range(FC):
                await_copy(o_slot(a, k, i), r_o.at[a, k, i])

    def project(i, first):
        a = lax.rem(first + i, Y * C)
        acc[...] += dot_t(tb[:, pl.ds(pl.multiple_of(a * cw, cw), cw)], oc[a])
        return first
    for a in (y * C, y * C + 1, yy(Y - 1) * C + 1, yy(1) * C):
        take(a)
    lax.fori_loop(0, 3 * C, project, yy(Y - 1) * C)
    take(yy(2) * C)
    take(yy(2) * C + 1)
    lax.fori_loop(0, C, project, yy(2) * C)
    out_ref[...] = acc[...].astype(jnp.bfloat16)

    def sent(ref, sem):
        pltpu.make_async_copy(ref, ref, sem).wait()
    sent(zb.at[pl.ds(0, Z - 1)], s_z)
    sent(zb.at[pl.ds(0, Z // 2)], s_x)

    @pl.when(own_core == c)
    def _():
        sent(zb.at[pl.ds(0, L * 3 // LL)], s_m)

    half_copy.wait_send()
    for k in range(1, Y):
        sent(yr.at[k], s_y.at[k])
        sent(yr.at[k], s_g.at[k])
        sent(xr.at[k], s_q.at[k])
    for k in range(Y):
        sent(yr.at[0], s_h.at[k])
    for k in range(4):
        sent(t4.at[0], s_t.at[k])
    sent(tb.at[pl.ds(0, H * rows), :], s_u.at[1])
    sent(tblk(mine), s_u.at[2])
    sent(tb.at[pl.ds(0, H * rows), :], s_u.at[3])
    sent(thalf(mine, 0), s_u.at[X])
    sent(thalf(mine, 1), s_u.at[X + 1])
    sent(tb.at[pl.ds(0, X * H * rows), :], s_u.at[0])
    sent(ob, s_o.at[0])
    sent(ob, s_o.at[1])
    sent(ob.at[pl.ds(0, L // 2)], s_c)
    sent(ob, s_r)
    def line(q, _):
        @pl.when((l < L - 1) & (q <= l))
        def _():
            sent(ob.at[q], s_l.at[0, q])

        @pl.when((l > 0) & (q >= l))
        def _():
            sent(ob.at[q], s_l.at[1, q])

        return 0

    lax.fori_loop(0, L, line, 0)


def on_device(tokens, weight):
    rows, d = tokens.shape
    rb, cb = weight.shape
    cw, r, half = LL * cb, rb // LL, H
    dma = pltpu.SemaphoreType.DMA
    bf, f32 = jnp.bfloat16, jnp.float32
    return pl.pallas_call(
        kernel,
        out_shape=jax.ShapeDtypeStruct((B * rows, rb), bf),
        in_specs=[pl.BlockSpec(memory_space=pl.ANY)] * 2,
        out_specs=pl.BlockSpec(memory_space=pltpu.VMEM),
        scratch_shapes=[
            pltpu.VMEM((Z, NC, rb // NC, cb), bf),
            pltpu.VMEM((H * C, rb, cw), bf),
            pltpu.VMEM((X * r, cw), bf),
            pltpu.VMEM((B * rows, d), bf),
            pltpu.VMEM((2, rows // 2, d), bf),
            pltpu.VMEM((H * C, X * r, rb), f32),
            pltpu.VMEM((half, X * r, rb), f32),
            pltpu.VMEM((half, X * r, rb), bf),
            pltpu.VMEM((Y, half, r, rb), bf),
            pltpu.VMEM((H * C, X * r, rb), bf),
            pltpu.VMEM((X * r, cw), f32),
            pltpu.VMEM((X * r, cw), bf),
            pltpu.VMEM((X, r, cw), bf),
            pltpu.VMEM((L, FC, r // FC, cw), bf),
            pltpu.VMEM((Y * C, rb, cw), bf),
            pltpu.VMEM((B * rows, rb), f32),
            dma((NC + 1,)),
            dma, dma((Z, NC)), dma, dma, dma((X, LL)), dma((H * C, NC, LL)),
            dma, dma, dma((Y,)), dma((Y,)), dma((Y,)), dma((Y,)), dma((C, Y)), dma((X,)), dma((X,)),
            dma((2, L)), dma((L, FC)), dma((2,)), dma, dma, dma((Y * C, LL, FC)),
            dma((4,)), dma((2,)), dma((2,)), dma((X + 2,)), dma((B,)),
        ],
        compiler_params=pltpu.CompilerParams(
            collective_id=0, has_side_effects=True, vmem_limit_bytes=64_000_000
        ),
        name="bjorck",
    )(tokens, weight)


def solution(mesh):
    placed = (P(("dp", "tensor"), None), P("tensor", "dp"))
    return jax.shard_map(
        on_device, mesh=mesh, in_specs=placed, out_specs=P("dp", "tensor"), check_vma=False
    )
```

```python
import functools

import jax
import jax.numpy as jnp
from jax import lax
from jax.experimental import pallas as pl
from jax.experimental.pallas import tpu as pltpu
from jax.sharding import PartitionSpec as P

MESH = pl.DeviceIdType.MESH
X, Y, H, L, C = 4, 4, 2, 8, 2
Z = H * L
B = X * H * C
LL = L // C
NC, FC = 2, 4


def dot_t(a, b):
    return lax.dot_general(a, b, (((1,), (1,)), ((), ())), preferred_element_type=jnp.float32)


def kernel(
    t_ref, w_ref, out_ref,
    zb, wc, rr, tb, t4, pf, pr, ys, yr, gb, po, xb, xr, ob, oc, acc,
    loc, s_z, r_z, s_x, s_m, r_m, r_w, s_p, r_p, s_y, r_y, s_g, s_h, r_g, s_q, r_q,
    s_l, r_l, s_o, s_c, s_r, r_o, s_t, r_t4, r_tp, s_u, r_t,
):
    dp, tn = lax.axis_index("dp"), lax.axis_index("tensor")
    y, l = lax.div(dp, L), lax.rem(dp, L)
    x, h, c = lax.div(tn, H * C), lax.rem(lax.div(tn, C), H), lax.rem(tn, C)
    z = h * L + l
    other = 1 - c
    rb, cb = w_ref.shape
    rows = t_ref.shape[0]
    cw = LL * cb
    r = rb // LL
    zr, fr, tr = rb // NC, r // FC, rows // 2

    def dev(ax, ay, az, ac):
        return (ay * L + lax.rem(az, L), (ax * H + lax.div(az, L)) * C + ac)

    def xs(k):
        return lax.rem(x + k, X)

    def yy(k):
        return lax.rem(y + k, Y)

    def zz(k):
        return lax.rem(z + k, Z)

    def send(src, dst, ssem, rsem, device):
        return pltpu.make_async_remote_copy(
            src_ref=src, dst_ref=dst, send_sem=ssem, recv_sem=rsem, device_id=device, device_id_type=MESH
        )

    def await_copy(ref, sem):
        pltpu.make_async_copy(ref, ref, sem).wait()

    def blk(ax, ah, ac):
        return (ax * H + ah) * C + ac

    def tblk(b):
        return tb.at[pl.ds(pl.multiple_of(b * rows, rows), rows), :]

    def thalf(b, i):
        return tb.at[pl.ds(pl.multiple_of(b * rows + i * tr, tr), tr), :]

    def part(ref, i):
        return ref.at[pl.ds(pl.multiple_of(i * r, r), r), :]

    mine, partner = blk(x, h, c), blk(x, 1 - h, c)
    loads = [pltpu.make_async_copy(w_ref.at[pl.ds(i * zr, zr), :], zb.at[z, i], loc.at[i]) for i in range(NC)]
    loads.append(pltpu.make_async_copy(t_ref, tblk(mine), loc.at[NC]))
    for load in loads:
        load.start()

    barrier = pltpu.get_barrier_semaphore()
    peers = [dev(x, y, zz(k), c) for k in (1, 2, Z - 2, Z - 1)] + [dev(x, y, z, other)]
    peers += [dev(xs(k), y, z, a) for k in (1, 2, 3) for a in (c, other)]
    peers += [dev(x, yy(k), z, a) for k in (1, 2, 3) for a in (c, other)]
    for peer in peers:
        pl.semaphore_signal(barrier, inc=1, device_id=peer, device_id_type=MESH)
    pl.semaphore_wait(barrier, len(peers))
    for load in loads:
        load.wait()

    own_core, own_row = lax.div(l, LL), lax.rem(l, LL) * r
    own_chunk = lax.div(own_row, zr)

    def slot(b, i, k):
        return wc.at[b, pl.ds(i * zr, zr), pl.ds(pl.multiple_of(k * cb, cb), cb)]

    def go(q, i, k):
        send(zb.at[q, i], zb.at[q, i], s_z, r_z.at[q, i], dev(x, y, zz(k % Z), c)).start()

    def spread(q, i):
        lq, hq = lax.rem(q, L), lax.div(q, L)
        to, k = lax.div(lq, LL), lax.rem(lq, LL)
        b = hq * C + c

        @pl.when((hq == h) & (own_core == c) & (own_chunk == i))
        def _():
            src = zb.at[q, i, pl.ds(pl.multiple_of(own_row - i * zr, r), r), :]
            dst = rr.at[pl.ds(pl.multiple_of(x * r, r), r), pl.ds(pl.multiple_of(k * cb, cb), cb)]
            for n in (2, 1, 3):
                send(src, dst, s_m, r_m.at[x, k], dev(xs(n), y, z, to)).start()

        @pl.when(to != c)
        def _():
            send(zb.at[q, i], slot(b, i, k), s_x, r_w.at[b, i, k], dev(x, y, z, other)).start()

        @pl.when(to == c)
        def _():
            pltpu.make_async_copy(zb.at[q, i], slot(b, i, k), r_w.at[b, i, k]).start()

    def t_spread(b, to):
        for n in to:
            send(tblk(b), tblk(b), s_u.at[n], r_t.at[b], dev(xs(n), y, z, c)).start()

    def t_other(b):
        send(tblk(b), tblk(b), s_u.at[0], r_t.at[b], dev(x, y, z, other)).start()

    def t_arrived(b):
        await_copy(tblk(b), r_t.at[b])
        t_other(b)
    for k in (2, 1):
        for i in range(NC):
            go(z, i, k)
            go(z, i, -k)
    for i in range(NC):
        spread(z, i)
    t_spread(mine, (2, 1, 3))
    t_other(mine)

    for n in range(1, Z // 2):
        for i in range(NC):
            for way in (1, -1):
                q = zz((-way * n) % Z)
                await_copy(zb.at[q, i], r_z.at[q, i])
                if n in (2, 4):
                    for k in (2, 1):
                        go(q, i, way * k)
                if n == 6:
                    if (way == 1) == (i < NC // 2):
                        go(q, i, way * 2)
                    go(q, i, way)
                spread(q, i)
    quarter = Z // 4
    send(thalf(mine, 0), t4.at[0], s_t.at[0], r_t4.at[0], dev(x, y, zz(quarter), c)).start()
    send(thalf(mine, 1), t4.at[1], s_t.at[1], r_t4.at[1], dev(x, y, zz(Z - quarter), c)).start()
    q = zz(Z // 2)
    for i in range(NC):
        await_copy(zb.at[q, i], r_z.at[q, i])
        spread(q, i)
    for b in range(H * C):
        for i in range(NC):
            for k in range(LL):
                await_copy(slot(b, i, k), r_w.at[b, i, k])
    for n in (1, 2, 3):
        for k in range(LL):
            await_copy(
                rr.at[pl.ds(pl.multiple_of(xs(n) * r, r), r), pl.ds(k * cb, cb)], r_m.at[xs(n), k]
            )

    half = H * C // C
    wr = wc[h * C + own_core, pl.ds(pl.multiple_of(own_row, r), r), :]
    rr[pl.ds(pl.multiple_of(x * r, r), r), :] = wr
    for i in range(half):
        b = other * half + i
        pf[b] = dot_t(rr[...], wc[b])
    half_copy = send(pf.at[pl.ds(other * half, half)], pr, s_p, r_p, dev(x, y, z, other))
    half_copy.start()
    for i in range(half):
        b = c * half + i
        pf[b] = dot_t(rr[...], wc[b])
    half_copy.wait_recv()
    for i in range(half):
        total = pf[c * half + i] + pr[i]
        pf[c * half + i] = total
        ys[i] = total.astype(jnp.bfloat16)

    def y_part(ref, k):
        return ref.at[:, pl.ds(pl.multiple_of(k * r, r), r), :]

    for k in (2, 1, Y - 1):
        send(y_part(ys, yy(k)), yr.at[k], s_y.at[k], r_y.at[k], dev(x, yy(k), z, c)).start()
    for k in (1, Y - 1, 2):
        await_copy(yr.at[k], r_y.at[k])
    my_rows = pl.ds(pl.multiple_of(y * r, r), r)
    for n in (1, 3, 2):
        t_arrived(blk(xs(n), h, c))
    for i in range(half):
        total = pf[c * half + i, my_rows, :]
        for k in range(1, Y):
            total = total + yr[k, i].astype(jnp.float32)
        gb[c * half + i, my_rows, :] = total.astype(jnp.bfloat16)

    def g_at(a, k):
        return gb.at[pl.ds(a * half, half), pl.ds(pl.multiple_of(k * r, r), r), :]
    for k in (2, 1, Y - 1):
        send(g_at(c, y), g_at(c, y), s_g.at[k], r_g.at[c, y], dev(x, yy(k), z, c)).start()
    send(g_at(c, y), g_at(c, y), s_h.at[0], r_g.at[c, y], dev(x, y, z, other)).start()
    for k in (1, Y - 1, 2):
        await_copy(g_at(c, yy(k)), r_g.at[c, yy(k)])
        send(g_at(c, yy(k)), g_at(c, yy(k)), s_h.at[k], r_g.at[c, yy(k)], dev(x, y, z, other)).start()
    for i, ahead, back in ((0, quarter, Z - quarter), (1, Z - quarter, quarter)):
        await_copy(t4.at[i], r_t4.at[i])
        home = blk(x, lax.div(zz(back), L), c)
        send(t4.at[i], thalf(home, i), s_t.at[2 + i], r_tp.at[i], dev(x, y, zz(ahead), c)).start()
    for k in range(Y):
        await_copy(g_at(other, yy(k)), r_g.at[other, yy(k)])

    total = jnp.dot(gb[0], wc[0], preferred_element_type=jnp.float32)
    for b in range(1, H * C):
        total = total + jnp.dot(gb[b], wc[b], preferred_element_type=jnp.float32)
    total = -0.5 * total
    po[...] = total
    xb[...] = total.astype(jnp.bfloat16)
    for n in (2, 1, 3):
        send(part(xb, xs(n)), xr.at[n], s_q.at[n], r_q.at[n], dev(xs(n), y, z, c)).start()
    for n in (1, 3, 2):
        await_copy(xr.at[n], r_q.at[n])
    total = 1.5 * wr.astype(jnp.float32) + po[pl.ds(pl.multiple_of(x * r, r), r), :]
    for n in (1, 2, 3):
        total = total + xr[n].astype(jnp.float32)
    for i in range(FC):
        ob[l, i] = total[i * fr:(i + 1) * fr].astype(jnp.bfloat16)

    def o_slot(a, k, i):
        return oc.at[a, pl.ds(pl.multiple_of(k * r + i * fr, fr), fr), :]

    def o_up(q, i):
        @pl.when(l < L - 1)
        def _():
            send(ob.at[q, i], ob.at[q, i], s_l.at[0, q], r_l.at[q, i], (dp + 1, tn)).start()

    def o_down(q, i):
        @pl.when(l > 0)
        def _():
            send(ob.at[q, i], ob.at[q, i], s_l.at[1, q], r_l.at[q, i], (dp - 1, tn)).start()

    def o_spread(q, i):
        to, k = lax.div(q, LL), lax.rem(q, LL)
        a = y * C + c
        dst, sem = o_slot(a, k, i), r_o.at[a, k, i]
        send(ob.at[q, i], dst, s_o.at[0], sem, dev(x, yy(1), z, to)).start()
        send(ob.at[q, i], dst, s_o.at[1], sem, dev(x, yy(Y - 1), z, to)).start()

        @pl.when(to != c)
        def _():
            send(ob.at[q, i], dst, s_c, sem, dev(x, y, z, other)).start()

        @pl.when(to == c)
        def _():
            pltpu.make_async_copy(ob.at[q, i], dst, sem).start()

    def o_relay(q):
        @pl.when(lax.div(q, LL) == c)
        def _():
            k = lax.rem(q, LL)
            for i in range(FC):
                for a, far in ((yy(Y - 1) * C, yy(1)), (yy(1) * C + 1, yy(Y - 1))):
                    await_copy(o_slot(a, k, i), r_o.at[a, k, i])
                    send(o_slot(a, k, i), o_slot(a, k, i), s_r, r_o.at[a, k, i], dev(x, far, z, c)).start()
    for i in range(FC):
        o_up(l, i)
        o_down(l, i)
    for i in range(FC):
        o_spread(l, i)

    def l_step(s, _):
        for i in range(FC):
            @pl.when(l - s >= 0)
            def _():
                await_copy(ob.at[l - s, i], r_l.at[l - s, i])
                o_up(l - s, i)
                o_spread(l - s, i)

            @pl.when(l + s < L)
            def _():
                await_copy(ob.at[l + s, i], r_l.at[l + s, i])
                o_down(l + s, i)
                o_spread(l + s, i)

        @pl.when(s == 2)
        def _():
            o_relay(l)

        @pl.when((s > 2) & (l - s + 2 >= 0))
        def _():
            o_relay(l - s + 2)

        @pl.when((s > 2) & (l + s - 2 < L))
        def _():
            o_relay(l + s - 2)

        @pl.when(s == 2)
        def _():
            await_copy(thalf(partner, 0), r_tp.at[0])
            await_copy(thalf(partner, 1), r_tp.at[1])
            t_spread(partner, (1, 3))
            t_other(partner)

        @pl.when(s == 5)
        def _():
            for i, near, far in ((0, xs(3), xs(1)), (1, xs(1), xs(3))):
                b = blk(near, 1 - h, c)
                await_copy(tblk(b), r_t.at[b])
                send(thalf(b, i), thalf(b, i), s_u.at[X + i], r_t.at[b], dev(far, y, z, c)).start()
                t_other(b)

        return 0
    lax.fori_loop(1, L, l_step, 0)
    for s in (L - 2, L - 1):
        @pl.when(l - s >= 0)
        def _():
            o_relay(l - s)

        @pl.when(l + s < L)
        def _():
            o_relay(l + s)
    t_arrived(blk(xs(2), 1 - h, c))
    for k in range(X):
        for hq in range(H):
            b = blk(xs(k), hq, other)
            await_copy(tblk(b), r_t.at[b])

    acc[...] = jnp.zeros_like(acc)

    def take(a):
        for k in range(LL):
            for i in range(FC):
                await_copy(o_slot(a, k, i), r_o.at[a, k, i])

    def project(i, first):
        a = lax.rem(first + i, Y * C)
        acc[...] += dot_t(tb[:, pl.ds(pl.multiple_of(a * cw, cw), cw)], oc[a])
        return first
    for a in (y * C, y * C + 1, yy(Y - 1) * C + 1, yy(1) * C):
        take(a)
    lax.fori_loop(0, 3 * C, project, yy(Y - 1) * C)
    take(yy(2) * C)
    take(yy(2) * C + 1)
    lax.fori_loop(0, C, project, yy(2) * C)
    out_ref[...] = acc[...].astype(jnp.bfloat16)

    def sent(ref, sem):
        pltpu.make_async_copy(ref, ref, sem).wait()
    sent(zb.at[pl.ds(0, Z - 1)], s_z)
    sent(zb.at[pl.ds(0, Z // 2)], s_x)

    @pl.when(own_core == c)
    def _():
        sent(zb.at[pl.ds(0, L * 3 // LL)], s_m)

    half_copy.wait_send()
    for k in range(1, Y):
        sent(yr.at[k], s_y.at[k])
        sent(yr.at[k], s_g.at[k])
        sent(xr.at[k], s_q.at[k])
    for k in range(Y):
        sent(yr.at[0], s_h.at[k])
    for k in range(4):
        sent(t4.at[0], s_t.at[k])
    sent(tb.at[pl.ds(0, H * rows), :], s_u.at[1])
    sent(tblk(mine), s_u.at[2])
    sent(tb.at[pl.ds(0, H * rows), :], s_u.at[3])
    sent(thalf(mine, 0), s_u.at[X])
    sent(thalf(mine, 1), s_u.at[X + 1])
    sent(tb.at[pl.ds(0, X * H * rows), :], s_u.at[0])
    sent(ob, s_o.at[0])
    sent(ob, s_o.at[1])
    sent(ob.at[pl.ds(0, L // 2)], s_c)
    sent(ob, s_r)
    def line(q, _):
        @pl.when((l < L - 1) & (q <= l))
        def _():
            sent(ob.at[q], s_l.at[0, q])

        @pl.when((l > 0) & (q >= l))
        def _():
            sent(ob.at[q], s_l.at[1, q])

        return 0

    lax.fori_loop(0, L, line, 0)


def on_device(tokens, weight):
    rows, d = tokens.shape
    rb, cb = weight.shape
    cw, r, half = LL * cb, rb // LL, H
    dma = pltpu.SemaphoreType.DMA
    bf, f32 = jnp.bfloat16, jnp.float32
    return pl.pallas_call(
        kernel,
        out_shape=jax.ShapeDtypeStruct((B * rows, rb), bf),
        in_specs=[pl.BlockSpec(memory_space=pl.ANY)] * 2,
        out_specs=pl.BlockSpec(memory_space=pltpu.VMEM),
        scratch_shapes=[
            pltpu.VMEM((Z, NC, rb // NC, cb), bf),
            pltpu.VMEM((H * C, rb, cw), bf),
            pltpu.VMEM((X * r, cw), bf),
            pltpu.VMEM((B * rows, d), bf),
            pltpu.VMEM((2, rows // 2, d), bf),
            pltpu.VMEM((H * C, X * r, rb), f32),
            pltpu.VMEM((half, X * r, rb), f32),
            pltpu.VMEM((half, X * r, rb), bf),
            pltpu.VMEM((Y, half, r, rb), bf),
            pltpu.VMEM((H * C, X * r, rb), bf),
            pltpu.VMEM((X * r, cw), f32),
            pltpu.VMEM((X * r, cw), bf),
            pltpu.VMEM((X, r, cw), bf),
            pltpu.VMEM((L, FC, r // FC, cw), bf),
            pltpu.VMEM((Y * C, rb, cw), bf),
            pltpu.VMEM((B * rows, rb), f32),
            dma((NC + 1,)),
            dma, dma((Z, NC)), dma, dma, dma((X, LL)), dma((H * C, NC, LL)),
            dma, dma, dma((Y,)), dma((Y,)), dma((Y,)), dma((Y,)), dma((C, Y)), dma((X,)), dma((X,)),
            dma((2, L)), dma((L, FC)), dma((2,)), dma, dma, dma((Y * C, LL, FC)),
            dma((4,)), dma((2,)), dma((2,)), dma((X + 2,)), dma((B,)),
        ],
        compiler_params=pltpu.CompilerParams(
            collective_id=0, has_side_effects=True, vmem_limit_bytes=64_000_000
        ),
        name="bjorck",
    )(tokens, weight)


def solution(mesh):
    placed = (P(("dp", "tensor"), None), P("tensor", "dp"))
    return jax.shard_map(
        on_device, mesh=mesh, in_specs=placed, out_specs=P("dp", "tensor"), check_vma=False
    )
```
